32 devices in a mesh: dp: 8 (over y, x, core), expert: 4 (over z).
Axes of the slice: x: 2, y: 2, z: 4, core: 2. Of those that a mesh axis runs over, the one named last changes fastest.
Arguments:
- tokens: bfloat16 [4096, 4096], P(('dp', 'expert')), may hold values from -6 to 6
- probs: bfloat16 [4096, 1], P(('dp', 'expert')), may hold values from 0.19921875 to 1
- routes: int32 [4096, 1], P(('dp', 'expert')), may hold values from 0 to 3; in each aligned block of 128 rows (0 to 127, 128 to 255, ...) at most 34 rows name the same one
- w_gate: bfloat16 [4, 4096, 1024], P('expert', 'dp'), may hold values from -0.09375 to 0.09375
- w_up: bfloat16 [4, 4096, 1024], P('expert', 'dp'), may hold values from -0.09375 to 0.09375
- w_down: bfloat16 [4, 1024, 4096], P('expert', None, 'dp'), may hold values from -0.1875 to 0.1875
- cotangent: bfloat16 [4096, 4096], P(('dp', 'expert')), may hold values from -6 to 6
Outputs:
- mixed: bfloat16 [4096, 4096], P(('dp', 'expert'))
- input_grad: bfloat16 [4096, 4096], P(('dp', 'expert'))
- grad_gate: bfloat16 [4, 4096, 1024], P('expert', 'dp')
- grad_up: bfloat16 [4, 4096, 1024], P('expert', 'dp')
- grad_down: bfloat16 [4, 1024, 4096], P('expert', None, 'dp')
The draws below stay inside these ranges and needn't reach their ends.
Inputs may be any that keep to these rules, and one draw needn't show every extreme that they name: `routes`: each row names exactly one expert. Among the 128 rows of one device (aligned blocks), no expert is named more than 34 times, a bound that some block reaches.
All inputs are finite; a program needn't handle non-finite values.
Results may differ from the reference program's by a relative error of at most 0.025.
Values may be sent and summed in bfloat16 or wider, within the bound.
A program may use at most 128 MiB of HBM per device.

```python
import math
import jax
import jax.numpy as jnp
import numpy as np
from jax import lax

D = 4096
FF = 1024
TOP = 1
TOK_DEV = 128
EXPERTS = 4
CAP = 34
TOKENS = 4096
N_DP = 8
N_EXPERT = 4


def block_levels(stream_key, extent, pieces, least, largest):
    gain = 1.0
    for axis_at, shards_of in pieces:
        heights = jax.random.uniform(jax.random.fold_in(jax.random.fold_in(stream_key, 6), axis_at), (shards_of,), jnp.float32, least / len(pieces), largest / len(pieces))
        gain = gain * jnp.repeat(jnp.exp(heights), extent[axis_at] // shards_of).reshape((-1,) + (1,) * (len(extent) - 1 - axis_at))
    return gain


def shared_out(own_key, own, number, rows, count, top, most, lean):
    ranking = jax.random.permutation(own_key, count)
    packed, usual = shares(count, rows * top, most, lean, True), shares(count, rows * top, most, lean, False)
    places = jnp.arange(count)

    def named(sizes, rotation):
        used = int((sizes > 0).sum())
        fixed = max(1, used // 4)
        shifted = fixed + (places - fixed + rotation * (used - fixed)) % max(1, count - fixed)
        return jnp.zeros((count,), jnp.int32).at[ranking[jnp.where(places < fixed, places, shifted)]].set(jnp.asarray(sizes, jnp.int32))

    sizes = jnp.where(number % 4 == 0, named(packed, number // 4), named(usual, number - number // 4 - 1))
    mixed = jax.random.permutation(jax.random.fold_in(own, 3), count)
    giver, receiver = mixed[0:count // 2 * 2:2], mixed[1:count // 2 * 2:2]
    room = jnp.minimum(sizes[giver] - 1, most - sizes[receiver]) // 2
    room = jnp.where((giver == ranking[0]) | (receiver == ranking[0]) | (sizes[receiver] == 0), 0, jnp.maximum(room, 0))
    shifted = jax.random.randint(jax.random.fold_in(own, 4), (count // 2,), 0, 1 << 20) % (room + 1)
    sizes = sizes.at[giver].add(-shifted).at[receiver].add(shifted)
    labels = jnp.searchsorted(jnp.cumsum(sizes), jnp.arange(rows * top), side="right").astype(jnp.int32)
    listing = labels.reshape(top, rows).T
    listing = listing[jax.random.permutation(jax.random.fold_in(own, 1), rows)]
    rotation = jax.random.randint(jax.random.fold_in(own, 2), (rows, 1), 0, top)
    return jnp.take_along_axis(listing, (jnp.arange(top)[None, :] + rotation) % top, axis=1)


def shares(number_of, total, reach, lean, full):
    loads = [(1 << 20) // math.isqrt(grade ** lean) + 1 for grade in range(1, number_of + 1)]
    largest = reach if full else min(reach, max(-(-total // number_of), total * loads[0] // sum(loads)))
    least = 1 if total - largest >= number_of - 1 else 0
    holding, rest = [largest] + [least] * (number_of - 1), total - largest - least * (number_of - 1)
    while rest > 0:
        free = [i for i in range(1, number_of) if holding[i] < largest] or [i for i in range(1, number_of) if holding[i] < reach]
        whole, left = sum([loads[i] for i in free]), rest
        for i in free:
            extra = min(reach - holding[i], max(1, left * loads[i] // whole), rest)
            holding[i] = holding[i] + extra
            rest = rest - extra
    return np.array(holding)


def centred(rng, shape, scale, bound, shards=(), held_as=jnp.bfloat16):
    loudness = block_levels(rng, shape, shards, -0.22, 0.18) if shards else 1.0
    values = jax.random.normal(rng, shape, jnp.float32) * scale * loudness
    return jnp.minimum(jnp.maximum(values, -bound), bound).astype(held_as)


def setup_inputs(seed: int = 0) -> dict:
    seeds = jax.random.split(jax.random.key(seed), 8)
    tokens = centred(seeds[0], (TOKENS, D), 1.0, 6.0, ((0, 32),))
    probs = jnp.clip(jnp.exp(math.log(1.0) - 1.6133518 * jax.random.uniform(seeds[1], (TOKENS, TOP), jnp.float32) ** block_levels(seeds[1], (TOKENS, TOP), ((0, 32),), -0.2, 0.2)), 0.19921875, 1.0).astype(jnp.bfloat16)
    routes_keys = jax.random.split(jax.random.fold_in(seeds[2], 1), TOKENS // TOK_DEV)
    routes_turns = jax.random.permutation(jax.random.fold_in(seeds[2], 3), TOKENS // TOK_DEV)
    routes = jax.vmap(lambda own, number: shared_out(jax.random.fold_in(seeds[2], 2), own, number, TOK_DEV, EXPERTS, TOP, CAP, 2))(routes_keys, routes_turns).reshape((TOKENS, TOP))
    w_gate = centred(seeds[3], (EXPERTS, D, FF), D ** -0.5, 0.09375, ((0, 4), (1, 8)))
    w_up = centred(seeds[4], (EXPERTS, D, FF), D ** -0.5, 0.09375, ((0, 4), (1, 8)))
    w_down = centred(seeds[5], (EXPERTS, FF, D), FF ** -0.5, 0.1875, ((0, 4), (2, 8)))
    cotangent = centred(seeds[6], (TOKENS, D), 1.0, 6.0, ((0, 32),))
    return dict(tokens=tokens, probs=probs, routes=routes, w_gate=w_gate, w_up=w_up, w_down=w_down, cotangent=cotangent)


def split_sum(left, right):
    parts = jnp.einsum("rnk,nkf->nrf", left.astype(jnp.float32), right.astype(jnp.float32),
                       precision=lax.Precision.HIGHEST)
    rounded = lax.optimization_barrier(parts.astype(jnp.bfloat16))
    return jnp.sum(rounded.astype(jnp.float32), axis=0)


def reference(tokens, probs, routes, w_gate, w_up, w_down, cotangent):
    flat_route = routes.reshape(-1)
    flat_prob = probs.reshape(-1)
    most = N_DP * N_EXPERT * CAP
    slices = D // N_DP

    def one_expert(carry, expert):
        mixed_sum, input_sum = carry
        hit = flat_route == expert
        pick = jnp.nonzero(hit, size=most, fill_value=0)[0].astype(jnp.int32)
        valid = jnp.arange(most, dtype=jnp.int32) < jnp.sum(hit.astype(jnp.int32))
        keep = valid.astype(jnp.float32)
        owner = (pick // TOP).astype(jnp.int32)
        rows = tokens[owner] * valid[:, None].astype(jnp.bfloat16)
        weight = flat_prob[pick].astype(jnp.float32) * keep
        gate_w = lax.dynamic_index_in_dim(w_gate, expert, 0, keepdims=False)
        up_w = lax.dynamic_index_in_dim(w_up, expert, 0, keepdims=False)
        down_w = lax.dynamic_index_in_dim(w_down, expert, 0, keepdims=False)
        split_rows = rows.reshape(most, N_DP, slices)
        gate_pre = split_sum(split_rows, gate_w.reshape(N_DP, slices, FF))
        up_value = split_sum(split_rows, up_w.reshape(N_DP, slices, FF))
        sig = jax.nn.sigmoid(gate_pre)
        act = (gate_pre * sig * up_value).astype(jnp.bfloat16)
        result = jnp.dot(act, down_w, preferred_element_type=jnp.float32).astype(jnp.bfloat16)
        mixed_sum = mixed_sum.at[owner].add(result.astype(jnp.float32) * weight[:, None])
        dout = (cotangent[owner].astype(jnp.float32) * weight[:, None]).astype(jnp.bfloat16)
        grad_down = jnp.dot(act.T, dout, preferred_element_type=jnp.float32).astype(jnp.bfloat16)
        down_split = jnp.transpose(down_w.reshape(FF, N_DP, slices), (1, 2, 0))
        dact = split_sum(dout.reshape(most, N_DP, slices), down_split)
        dgate = (dact * up_value * sig * (1.0 + gate_pre * (1.0 - sig))).astype(jnp.bfloat16)
        dup = (dact * gate_pre * sig).astype(jnp.bfloat16)
        grad_gate = jnp.dot(rows.T, dgate, preferred_element_type=jnp.float32).astype(jnp.bfloat16)
        grad_up = jnp.dot(rows.T, dup, preferred_element_type=jnp.float32).astype(jnp.bfloat16)
        slot_grad = (jnp.dot(dgate, gate_w.T, preferred_element_type=jnp.float32)
                     + jnp.dot(dup, up_w.T, preferred_element_type=jnp.float32)).astype(jnp.bfloat16)
        input_sum = input_sum.at[owner].add(slot_grad.astype(jnp.float32) * keep[:, None])
        return (mixed_sum, input_sum), (grad_gate, grad_up, grad_down)

    start = (jnp.zeros((TOKENS, D), jnp.float32), jnp.zeros((TOKENS, D), jnp.float32))
    (mixed_sum, input_sum), grads = lax.scan(one_expert, start, jnp.arange(EXPERTS, dtype=jnp.int32))
    return (mixed_sum.astype(jnp.bfloat16), input_sum.astype(jnp.bfloat16), grads[0], grads[1], grads[2])
```

```python
import functools

import jax
import jax.numpy as jnp
from jax import lax
from jax.experimental import pallas as pl
from jax.experimental.pallas import tpu as pltpu
from jax.sharding import PartitionSpec as P

BF = jnp.bfloat16
F32 = jnp.float32


def nn(a, b):
    return lax.dot_general(a, b, (((1,), (0,)), ((), ())), preferred_element_type=F32)


def nt(a, b):
    return lax.dot_general(a, b, (((1,), (1,)), ((), ())), preferred_element_type=F32)


def tn(a, b):
    return lax.dot_general(a, b, (((0,), (0,)), ((), ())), preferred_element_type=F32)


def flat_bits(value):
    return value.bit_length() - 1


def layer_kernel(
    n, e_n, cap,
    tok, cot, route, prob, wg_h, wu_h, wd_h,
    mix_o, ig_o, gg_o, gu_o, gd_o,
    tab, tabw, pn, pnt, pe, pet, st, te, tiles, et, eb,
    xs, ds_, xr, dr, xp, dp, pwg, pwu, pwd,
    gs, gr, hs, hr, pre, upv, act, dga, dua, rs, ss, yb, sb, x_t, wg, wu, wd,
    sem_own, sem_pw, sem_out, sem_in, sem_back, sem_ext, sem_ps, sem_q,
):
    m = lax.axis_index("dp")
    z = lax.axis_index("expert")
    q_n = n // 2
    q = m // 2
    c = lax.rem(m, 2)
    pm = m + 1 - 2 * c
    slots = n * cap
    main = cap // 16 * 16
    extra = cap - main
    em, nm = e_n * main, n * main
    t_rows, w = tok.shape[0], tok.shape[1] // n
    cbs = w // 128
    ff = wg_h.shape[1]
    fh = ff // 2
    b = fh // q_n

    def span(start, size, unit):
        return pl.ds(pl.multiple_of(start, unit), size)

    def rows(k):
        return span(k * slots, slots, 16)

    def mains(k, i):
        return span(k * slots + i * main, main, 16)

    def chunk_mains(k):
        return span(k * slots, nm, 16)

    def chunk_extras(k):
        return span(k * slots + nm, 16, 16)

    def places(e):
        return span(e * main, main, 16)

    def cols(k):
        return span(k * w, w, 128)

    def lanes(k):
        return span(k * 128, 128, 128)

    def tile(k):
        return span(k * 16, 16, 16)

    my_half = span(c * fh, fh, 128)
    other_half = span((1 - c) * fh, fh, 128)

    def block(qq):
        return span(c * fh + qq * b, b, 128)

    def copy(src, dst, send, recv, dp_at, ex_at):
        return pltpu.make_async_remote_copy(
            src_ref=src, dst_ref=dst, send_sem=send, recv_sem=recv,
            device_id=(dp_at, ex_at), device_id_type=pl.DeviceIdType.MESH,
        )

    def near(d):
        upper = (2 * z) // e_n
        low = z + upper * (e_n - 1 - 2 * z)
        side = 2 * lax.rem(d, 2) - 1
        at = jnp.where(d <= 2 * low, low + side * ((d + 1) // 2), d)
        return at + upper * (e_n - 1 - 2 * at)

    def far(d):
        return near(e_n - 1 - d)

    def loop(lo, hi, body):
        def step(i, carry):
            body(i)
            return carry

        lax.fori_loop(lo, hi, step, 0)

    def partner(at, d, size):
        if size & (size - 1):
            return lax.rem(at + d, size)
        other, step = at, 1
        while step < size:
            if d & step:
                other = other + step - 2 * step * lax.rem(at // step, 2)
            step *= 2
        return other

    def q_others(body):
        for d in range(1, q_n):
            body(partner(q, d, q_n))

    def to_plane(e, pairs):
        @pl.when(e != z)
        def _():
            for out, _ in pairs:
                out(m, e).start()

        @pl.when(e == z)
        def _():
            for _, own in pairs:
                own.start()

        for d in range(1, n):
            for out, _ in pairs:
                out(partner(m, d, n), e).start()

    def x_out(i, e):
        return copy(xs.at[places(e), cols(i)], xr.at[mains(z, m), :], sem_out.at[0], sem_in.at[0, z], i, e)

    x_own = pltpu.make_async_copy(xs.at[places(z), cols(m)], xr.at[mains(z, m), :], sem_in.at[0, z])

    def d_out(i, e):
        return copy(ds_.at[places(e), cols(i)], dr.at[mains(z, m), :], sem_out.at[1], sem_in.at[1, z], i, e)

    d_own = pltpu.make_async_copy(ds_.at[places(z), cols(m)], dr.at[mains(z, m), :], sem_in.at[1, z])

    def t_out(i, e):
        return copy(te.at[tile(e), lanes(i)], tiles.at[z, tile(m), :], sem_out.at[2], sem_in.at[2, z], i, e)

    t_own = pltpu.make_async_copy(te.at[tile(z), lanes(m)], tiles.at[z, tile(m), :], sem_in.at[2, z])

    def y_out(i, k):
        return copy(rs.at[mains(k, i), :], yb.at[places(z), cols(m)], sem_out.at[3], sem_back.at[0, m], i, k)

    y_own = pltpu.make_async_copy(rs.at[mains(z, m), :], yb.at[places(z), cols(m)], sem_back.at[0, m])

    def s_out(i, k):
        return copy(ss.at[mains(k, i), :], sb.at[places(z), cols(m)], sem_out.at[4], sem_back.at[1, m], i, k)

    s_own = pltpu.make_async_copy(ss.at[mains(z, m), :], sb.at[places(z), cols(m)], sem_back.at[1, m])

    def e_out_(i, k):
        return copy(et.at[tile(k * n + i), :], eb.at[tile(z), lanes(m)], sem_out.at[5], sem_ext.at[0], i, k)

    e_own = pltpu.make_async_copy(et.at[tile(z * n + m), :], eb.at[tile(z), lanes(m)], sem_ext.at[0])

    def arrived(ref, sem):
        copy(ref, ref, sem, sem, pm, z).wait_recv()

    def sent(ref, sem):
        copy(ref, ref, sem, sem, pm, z).wait_send()

    def pass_pair(no, src, dst):
        def out(k):
            return copy(src(k), dst(k), sem_ps.at[2 * no, k], sem_ps.at[2 * no + 1, k], pm, z)

        return out

    xf = pass_pair(0, lambda k: xr.at[rows(k)], lambda k: xp.at[rows(k)])
    df = pass_pair(1, lambda k: dr.at[rows(k)], lambda k: dp.at[rows(k)])

    def half_pass(no, ref):
        send, recv = sem_ps.at[2 * no], sem_ps.at[2 * no + 1]

        def out(k):
            part = ref.at[rows(k), my_half]
            return copy(part, part, send.at[k], recv.at[k], pm, z)

        def got(k):
            part = ref.at[rows(k), other_half]
            return copy(part, part, send.at[k], recv.at[k], pm, z)

        return out, got

    af_out, af_got = half_pass(2, act)
    ef_out, ef_got = half_pass(3, dga)
    uf_out, uf_got = half_pass(4, dua)

    def q_pair(no, src, dst):
        def out(k, i):
            return copy(src(k, i), dst(k, q), sem_q.at[2 * no, k, i], sem_q.at[2 * no + 1, k, q], 2 * i + c, z)

        def got(k, i):
            return copy(src(k, i), dst(k, i), sem_q.at[2 * no, k, i], sem_q.at[2 * no + 1, k, i], 2 * i + c, z)

        return out, got

    g_out, g_got = q_pair(0, lambda k, i: gs.at[k, i], lambda k, i: gr.at[k, i])
    h_out, h_got = q_pair(1, lambda k, i: hs.at[k, i], lambda k, i: hr.at[k, i])

    def share_pair(no, ref):
        def out(k, i):
            part = ref.at[rows(k), block(q)]
            return copy(part, part, sem_q.at[2 * no, k, i], sem_q.at[2 * no + 1, k, q], 2 * i + c, z)

        def got(k, i):
            part = ref.at[rows(k), block(i)]
            return copy(part, part, sem_q.at[2 * no, k, i], sem_q.at[2 * no + 1, k, i], 2 * i + c, z)

        return out, got

    a_out, a_got = share_pair(2, act)
    e_out, e_got = share_pair(3, dga)
    u_out, u_got = share_pair(4, dua)
    pw = [
        copy(wg_h.at[:, other_half], pwg, sem_pw.at[0, 0], sem_pw.at[1, 0], pm, z),
        copy(wu_h.at[:, other_half], pwu, sem_pw.at[0, 1], sem_pw.at[1, 1], pm, z),
        copy(wd_h.at[other_half], pwd, sem_pw.at[0, 2], sem_pw.at[1, 2], pm, z),
    ]
    own = [
        pltpu.make_async_copy(src, dst, sem_own.at[i])
        for i, (src, dst) in enumerate(((wg_h, wg), (wu_h, wu), (wd_h, wd)))
    ]
    for one in own:
        one.start()
    barrier = pltpu.get_barrier_semaphore()
    here = m * e_n + z

    def greet(d):
        other = lax.rem(here + d, n * e_n)
        pl.semaphore_signal(
            barrier, inc=1, device_id=(other // e_n, lax.rem(other, e_n)),
            device_id_type=pl.DeviceIdType.MESH,
        )

    loop(1, n * e_n, greet)

    name = route[...]
    share = prob[...].astype(F32)
    hits = jnp.where(lax.broadcasted_iota(jnp.int32, (16, t_rows), 0) == name, 1.0, 0.0)
    earlier = jnp.where(
        lax.broadcasted_iota(jnp.int32, (t_rows, t_rows), 0)
        < lax.broadcasted_iota(jnp.int32, (t_rows, t_rows), 1), 1.0, 0.0,
    ).astype(BF)
    place = jnp.sum(nn(hits.astype(BF), earlier) * hits, axis=0, keepdims=True).astype(jnp.int32)
    target = jnp.where(
        place < main, name * main + place, em + name * extra + place - main
    )
    hit = lax.broadcasted_iota(jnp.int32, (em + 16, t_rows), 0) == target
    tab[...] = jnp.where(hit, 1.0, 0.0).astype(BF)
    tabw[...] = jnp.where(hit, share, 0.0).astype(BF)

    def packing(count, flip):
        shape = (count * 16, 2 * cbs * 16) if flip else (2 * cbs * 16, count * 16)
        long = lax.broadcasted_iota(jnp.int32, shape, 1 if flip else 0)
        packed = lax.broadcasted_iota(jnp.int32, shape, 0 if flip else 1)
        slot = long & 15
        group = long >> 4
        want = ((slot >> flat_bits(extra)) << 4) + group * extra + (slot & (extra - 1))
        return jnp.where((packed == want) & (slot < count * extra), 1.0, 0.0).astype(BF)

    def gather(table, src, dst, a):
        for i in range(n):
            at = slice(i * w, (i + 1) * w)
            part = nn(table[...], src[:, at]).astype(BF)
            dst[:, at] = part[:em]
            for cb in range(cbs):
                g = (a * cbs + cb) * 16
                st[g:g + 16, i * 128:(i + 1) * 128] = part[em:, cb * 128:(cb + 1) * 128]

    gather(tab, tok, xs, 0)
    pl.semaphore_wait(barrier, n * e_n - 1)
    to_plane(z, [(x_out, x_own)])
    gather(tabw, cot, ds_, 1)
    pet[...] = packing(e_n, True)
    te[...] = nn(pet[...], st[...]).astype(BF)
    to_plane(z, [(t_out, t_own)])
    loop(1, e_n, lambda d: to_plane(near(d), [(x_out, x_own), (t_out, t_own)]))
    for one in pw:
        one.start()
    pn[...] = packing(n, False)
    pnt[...] = packing(n, True)
    pe[...] = packing(e_n, False)
    for one in own:
        one.wait()
    for one in pw:
        one.wait_recv()

    def gate_up(k):
        arrived(tiles.at[k], sem_in.at[2, k])
        spare = nn(pn[...], tiles[k]).astype(BF)
        for cb in range(cbs):
            at = slice(cb * 128, (cb + 1) * 128)
            xr[chunk_extras(k), at] = spare[cb * 16:(cb + 1) * 16]
            dr[chunk_extras(k), at] = spare[(cbs + cb) * 16:(cbs + cb + 1) * 16]
        arrived(xr.at[chunk_mains(k)], sem_in.at[0, k])
        xf(k).start()
        xf(k).wait_recv()
        for at, own_w, other_w in ((0, wg, pwg), (1, wu, pwu)):
            part = nn(xr[rows(k), :], own_w[:, my_half]) + nn(xp[rows(k), :], other_w[...])
            part = part.astype(BF)
            for i in range(q_n):
                gs[k, i, :, at * b:(at + 1) * b] = part[:, i * b:(i + 1) * b]
        q_others(lambda i: g_out(k, i).start())

    def dout_send(k):
        to_plane(k, [(d_out, d_own)])

    def activate(k):
        total = gs[k, q].astype(F32)
        for dd in range(1, q_n):
            i = partner(q, dd, q_n)
            g_got(k, i).wait_recv()
            total = total + gr[k, i].astype(F32)
        gate, up = total[:, :b], total[:, b:]
        pre[rows(k), :] = gate
        upv[rows(k), :] = up
        act[rows(k), block(q)] = (gate * jax.nn.sigmoid(gate) * up).astype(BF)
        q_others(lambda i: a_out(k, i).start())

    def act_pass(k):
        q_others(lambda i: a_got(k, i).wait_recv())
        af_out(k).start()

    def result_rows(k):
        af_got(k).wait_recv()
        rs[rows(k), :] = nn(act[rows(k), :], wd[...]).astype(BF)
        to_plane(k, [(y_out, y_own)])

    def down(k):
        arrived(dr.at[chunk_mains(k)], sem_in.at[1, k])
        df(k).start()
        df(k).wait_recv()
        part = nt(dr[rows(k), :], wd[my_half, :]) + nt(dp[rows(k), :], pwd[...])
        part = part.astype(BF)
        for i in range(q_n):
            hs[k, i] = part[:, i * b:(i + 1) * b]
        q_others(lambda i: h_out(k, i).start())

    def act_grad(k):
        total = hs[k, q].astype(F32)
        for dd in range(1, q_n):
            i = partner(q, dd, q_n)
            h_got(k, i).wait_recv()
            total = total + hr[k, i].astype(F32)
        gate, up = pre[rows(k), :], upv[rows(k), :]
        sig = jax.nn.sigmoid(gate)
        dga[rows(k), block(q)] = (total * up * sig * (1.0 + gate * (1.0 - sig))).astype(BF)
        dua[rows(k), block(q)] = (total * gate * sig).astype(BF)
        q_others(lambda i: e_out(k, i).start())
        q_others(lambda i: u_out(k, i).start())

    def handed(k):
        q_others(lambda i: e_got(k, i).wait_recv())
        ef_out(k).start()
        q_others(lambda i: u_got(k, i).wait_recv())
        uf_out(k).start()

    def input_grad(k):
        ef_got(k).wait_recv()
        uf_got(k).wait_recv()
        ss[rows(k), :] = (nt(dga[rows(k), :], wg[...]) + nt(dua[rows(k), :], wu[...])).astype(BF)
        to_plane(k, [(s_out, s_own)])
        long = [
            buf[chunk_extras(k), cb * 128:(cb + 1) * 128] for buf in (rs, ss) for cb in range(cbs)
        ]
        et[span(k * n * 16, n * 16, 16), :] = nn(pnt[...], jnp.concatenate(long, axis=0)).astype(BF)
        to_plane(k, [(e_out_, e_own)])

    stages = (
        (0, near, gate_up), (0, near, dout_send), (1, near, activate), (2, near, act_pass),
        (3, near, result_rows), (3, far, down), (5, far, act_grad), (6, far, handed), (7, far, input_grad),
    )

    def turn(t):
        for lag, order, body in stages:
            @pl.when((t >= lag) & (t < lag + e_n))
            def _():
                body(order(t - lag))

    loop(0, 7 + e_n, turn)

    x_t[...] = xr[...].T
    wide = 2 * b

    def down_grad(j):
        at = span(j * wide, wide, 128)
        gd_o[at, :] = tn(act[:, at], dr[...]).astype(BF)

    loop(0, ff // wide, down_grad)

    def weight_grad(j):
        at = span(j * wide, wide, 128)
        gg_o[:, at] = nn(x_t[...], dga[:, at]).astype(BF)
        gu_o[:, at] = nn(x_t[...], dua[:, at]).astype(BF)

    loop(0, ff // wide, weight_grad)

    arrived(eb, sem_ext.at[0])
    spare = nn(pe[...], eb[...]).astype(BF)
    for a, buf in ((0, yb), (1, sb)):
        for cb in range(cbs):
            g = (a * cbs + cb) * 16
            for i in range(n):
                buf[em:em + 16, i * w + cb * 128:i * w + (cb + 1) * 128] = spare[g:g + 16, i * 128:(i + 1) * 128]

    def combine(a, table, buf, out):
        def one(i):
            arrived(buf.at[0:em, cols(i)], sem_back.at[a, i])
            out[:, cols(i)] = tn(table[...], buf[:, cols(i)]).astype(BF)

        loop(0, n, one)

    combine(0, tabw, yb, mix_o)
    combine(1, tab, sb, ig_o)

    for at in (0, 1, 3, 4):
        sent(xr.at[0:(n * e_n - 1) * main], sem_out.at[at])
    for at in (2, 5):
        sent(et.at[0:(n * e_n - 1) * 16], sem_out.at[at])
    for one in pw:
        one.wait_send()

    def chunk_end(k):
        for out in (xf, df, af_out, ef_out, uf_out):
            out(k).wait_send()
        for out in (g_out, h_out, a_out, e_out, u_out):
            q_others(lambda i: out(k, i).wait_send())

    loop(0, e_n, chunk_end)


def fused_layer(tokens, probs, routes, w_gate, w_up, w_down, cotangent, n, e_n, cap):
    t_rows, width = tokens.shape
    w = width // n
    ff = w_gate.shape[2]
    slots, fh, q_n = n * cap, ff // 2, n // 2
    b = fh // q_n
    r = e_n * slots
    main = cap // 16 * 16
    tr, cbs = e_n * main + 16, w // 128
    long = 2 * cbs * 16
    vm = pl.BlockSpec(memory_space=pltpu.VMEM)

    def v(*shape, dtype=BF):
        return pltpu.VMEM(shape, dtype)

    scratch = [
        v(tr, t_rows), v(tr, t_rows), v(long, n * 16), v(n * 16, long), v(long, e_n * 16), v(e_n * 16, long),
        v(long, n * 128), v(e_n * 16, n * 128), v(e_n, n * 16, 128), v(e_n * n * 16, 128), v(e_n * 16, n * 128),
        v(e_n * main, width), v(e_n * main, width),
        v(r, w), v(r, w), v(r, w), v(r, w),
        v(w, fh), v(w, fh), v(fh, w),
        v(e_n, q_n, slots, 2 * b), v(e_n, q_n, slots, 2 * b),
        v(e_n, q_n, slots, b), v(e_n, q_n, slots, b),
        v(r, b, dtype=F32), v(r, b, dtype=F32),
        v(r, ff), v(r, ff), v(r, ff),
        v(r, w), v(r, w), v(tr, width), v(tr, width),
        v(w, r), v(w, ff), v(w, ff), v(ff, w),
        pltpu.SemaphoreType.DMA((3,)),
        pltpu.SemaphoreType.DMA((2, 3)),
        pltpu.SemaphoreType.DMA((6,)),
        pltpu.SemaphoreType.DMA((3, e_n)),
        pltpu.SemaphoreType.DMA((2, n)),
        pltpu.SemaphoreType.DMA((1,)),
        pltpu.SemaphoreType.DMA((10, e_n)),
        pltpu.SemaphoreType.DMA((10, e_n, q_n)),
    ]
    mixed, input_grad, gg, gu, gd = pl.pallas_call(
        functools.partial(layer_kernel, n, e_n, cap),
        out_shape=(
            jax.ShapeDtypeStruct((t_rows, width), BF),
            jax.ShapeDtypeStruct((t_rows, width), BF),
            jax.ShapeDtypeStruct((w, ff), BF),
            jax.ShapeDtypeStruct((w, ff), BF),
            jax.ShapeDtypeStruct((ff, w), BF),
        ),
        in_specs=[vm] * 4 + [pl.BlockSpec(memory_space=pl.ANY)] * 3,
        out_specs=(vm,) * 5,
        scratch_shapes=scratch,
        compiler_params=pltpu.CompilerParams(
            collective_id=0, has_side_effects=True, vmem_limit_bytes=62 * 1024 * 1024
        ),
    )(tokens, cotangent, routes.reshape(1, -1), probs.reshape(1, -1), w_gate[0], w_up[0], w_down[0])
    return mixed, input_grad, gg[None], gu[None], gd[None]


def packs(n, e_n, cap, width):
    extra, cbs = cap % 16, width // n // 128
    return (
        cap > 16 and extra > 0 and extra & (extra - 1) == 0 and n & (n - 1) == 0
        and n * extra == 16 and e_n * extra <= 16 and 2 * extra * cbs == 16
    )


def slot_table(routes, experts_all, capacity):
    flat = routes.reshape(-1)
    hits = (flat[:, None] == jnp.arange(experts_all, dtype=jnp.int32)[None, :]).astype(jnp.int32)
    at = jnp.arange(flat.shape[0], dtype=jnp.int32)
    earlier = (at[:, None] > at[None, :]).astype(BF)
    before = nn(earlier, hits.astype(BF)).astype(jnp.int32)
    place = jnp.sum(before * hits, axis=1)
    target = flat * capacity + place
    table = jnp.arange(experts_all * capacity, dtype=jnp.int32)[:, None] == target[None, :]
    return table.astype(jnp.bfloat16)


def spread_rows(table, values, slices):
    shaped = values.reshape(values.shape[0], slices, values.shape[1] // slices)
    return jnp.einsum("st,tnk->nsk", table, shaped, preferred_element_type=jnp.float32).astype(
        jnp.bfloat16
    )


def to_rows(received, local_count):
    sources, slots, width = received.shape
    shaped = received.reshape(sources, local_count, slots // local_count, width)
    shaped = jnp.swapaxes(shaped, 1, 2)
    return shaped.reshape(sources * (slots // local_count), local_count, width)


def to_sources(rowwise, capacity):
    total, local_count, width = rowwise.shape
    shaped = rowwise.reshape(total // capacity, capacity, local_count, width)
    shaped = jnp.swapaxes(shaped, 1, 2)
    return shaped.reshape(total // capacity, local_count * capacity, width)


def collect(table, back, tok_rows, top):
    picked = jnp.einsum("st,nsk->tnk", table, back, preferred_element_type=jnp.float32)
    return picked.reshape(tok_rows, top, -1)


def per_device(tokens, probs, routes, w_gate, w_up, w_down, cotangent):
    local_count = w_gate.shape[0]
    n_dp = lax.axis_size("dp")
    n_exp = lax.axis_size("expert")
    experts_all = local_count * n_exp
    tok_rows, width = tokens.shape
    top = routes.shape[1]
    capacity = max(2, 17 * tok_rows * top // (16 * experts_all))
    ff = w_gate.shape[2]
    if (
        local_count == 1 and top == 1 and n_dp % 2 == 0 and ff % (n_dp * 128) == 0
        and tok_rows % 128 == 0 and width % (n_dp * 128) == 0 and packs(n_dp, n_exp, capacity, width)
    ):
        return fused_layer(
            tokens, probs, routes, w_gate, w_up, w_down, cotangent, n_dp, n_exp, capacity
        )
    blocks = n_dp * n_exp
    slot_width = width // n_dp
    table = slot_table(routes, experts_all, capacity)
    x_send = spread_rows(table, jnp.repeat(tokens, top, axis=0), n_dp)
    x_send = x_send.reshape(blocks, local_count * capacity, slot_width)
    weight = probs.astype(jnp.float32)
    scaled = (jnp.repeat(cotangent, top, axis=0).astype(jnp.float32) * weight).astype(jnp.bfloat16)
    x_got = lax.all_to_all(x_send, ("dp", "expert"), split_axis=0, concat_axis=0, tiled=True)
    rows = to_rows(x_got, local_count)
    part = rows
    gate = jnp.einsum("red,edf->ref", part, w_gate, preferred_element_type=jnp.float32)
    upper = jnp.einsum("red,edf->ref", part, w_up, preferred_element_type=jnp.float32)
    summed = lax.psum_scatter(
        jnp.stack([gate, upper], axis=2).astype(jnp.bfloat16), "dp", scatter_dimension=0, tiled=True
    ).astype(jnp.float32)
    gate_pre = summed[:, :, 0]
    up_value = summed[:, :, 1]
    sig = jax.nn.sigmoid(gate_pre)
    act = (gate_pre * sig * up_value).astype(jnp.bfloat16)
    act_all = lax.all_gather(act, "dp", axis=0, tiled=True)
    result = jnp.einsum("ref,efd->red", act_all, w_down, preferred_element_type=jnp.float32).astype(
        jnp.bfloat16
    )
    outgoing = to_sources(result, capacity)
    back = lax.all_to_all(outgoing, ("dp", "expert"), split_axis=0, concat_axis=0, tiled=True)
    back = back.reshape(n_dp, experts_all * capacity, slot_width)
    picked = collect(table, back, tok_rows, top)
    mixed = jnp.sum(picked * weight[..., None], axis=1).astype(jnp.bfloat16)
    dy_send = spread_rows(table, scaled, n_dp).reshape(blocks, local_count * capacity, slot_width)
    dy_got = lax.all_to_all(dy_send, ("dp", "expert"), split_axis=0, concat_axis=0, tiled=True)
    dout = to_rows(dy_got, local_count)
    grad_down = jnp.einsum("ref,red->efd", act_all, dout, preferred_element_type=jnp.float32)
    part = dout
    dact = lax.psum_scatter(
        jnp.einsum("red,efd->ref", part, w_down, preferred_element_type=jnp.float32).astype(
            jnp.bfloat16
        ),
        "dp",
        scatter_dimension=0,
        tiled=True,
    ).astype(jnp.float32)
    dgate = (dact * up_value * sig * (1.0 + gate_pre * (1.0 - sig))).astype(jnp.bfloat16)
    dup = (dact * gate_pre * sig).astype(jnp.bfloat16)
    dgate_all, dup_all = (
        lax.all_gather(dgate, "dp", axis=0, tiled=True),
        lax.all_gather(dup, "dp", axis=0, tiled=True),
    )
    grad_gate = jnp.einsum("red,ref->edf", rows, dgate_all, preferred_element_type=jnp.float32)
    grad_up = jnp.einsum("red,ref->edf", rows, dup_all, preferred_element_type=jnp.float32)
    slot_grad = jnp.einsum(
        "ref,edf->red", dgate_all, w_gate, preferred_element_type=jnp.float32
    ) + jnp.einsum("ref,edf->red", dup_all, w_up, preferred_element_type=jnp.float32)
    slot_grad = slot_grad.astype(jnp.bfloat16)
    returned = lax.all_to_all(
        to_sources(slot_grad, capacity), ("dp", "expert"), split_axis=0, concat_axis=0, tiled=True
    )
    returned = returned.reshape(n_dp, experts_all * capacity, slot_width)
    input_grad = jnp.sum(collect(table, returned, tok_rows, top), axis=1).astype(jnp.bfloat16)
    return (
        mixed,
        input_grad,
        grad_gate.astype(jnp.bfloat16),
        grad_up.astype(jnp.bfloat16),
        grad_down.astype(jnp.bfloat16),
    )


def solution(mesh):
    return jax.shard_map(
        per_device,
        mesh=mesh,
        in_specs=(
            P(("dp", "expert"), None),
            P(("dp", "expert"), None),
            P(("dp", "expert"), None),
            P("expert", "dp", None),
            P("expert", "dp", None),
            P("expert", None, "dp"),
            P(("dp", "expert"), None),
        ),
        out_specs=(
            P(("dp", "expert"), None),
            P(("dp", "expert"), None),
            P("expert", "dp", None),
            P("expert", "dp", None),
            P("expert", None, "dp"),
        ),
        check_vma=False,
    )
```

```python
import functools

import jax
import jax.numpy as jnp
from jax import lax
from jax.experimental import pallas as pl
from jax.experimental.pallas import tpu as pltpu
from jax.sharding import PartitionSpec as P

BF = jnp.bfloat16
F32 = jnp.float32


def nn(a, b):
    return lax.dot_general(a, b, (((1,), (0,)), ((), ())), preferred_element_type=F32)


def nt(a, b):
    return lax.dot_general(a, b, (((1,), (1,)), ((), ())), preferred_element_type=F32)


def tn(a, b):
    return lax.dot_general(a, b, (((0,), (0,)), ((), ())), preferred_element_type=F32)


def flat_bits(value):
    return value.bit_length() - 1


def layer_kernel(
    n, e_n, cap,
    tok, cot, route, prob, wg_h, wu_h, wd_h,
    mix_o, ig_o, gg_o, gu_o, gd_o,
    tab, tabw, pn, pnt, pe, pet, st, te, tiles, et, eb,
    xs, ds_, xr, dr, xp, dp, pwg, pwu, pwd,
    gs, gr, gt, hst, hsb, hrt, hrb, htt, htb, dsum, pre, upv, act, dga, dua, rs, ss, yb, sb, x_t, wg, wu, wd,
    sem_own, sem_pw, sem_out, sem_in, sem_back, sem_ext, sem_ps, sem_q,
):
    m = lax.axis_index("dp")
    z = lax.axis_index("expert")
    q_n = n // 2
    q = m // 2
    c = lax.rem(m, 2)
    pm = m + 1 - 2 * c
    on_x, on_y = lax.rem(q, 2), q // 2
    qx, qy = q + 1 - 2 * on_x, q + 2 - 4 * on_y
    mx, my = 2 * qx + c, 2 * qy + c
    slots = n * cap
    top = (slots // 16 + 1) // 2 * 16
    bottom = slots - top
    main = cap // 16 * 16
    extra = cap - main
    em, nm = e_n * main, n * main
    t_rows, w = tok.shape[0], tok.shape[1] // n
    cbs = w // 128
    ff = wg_h.shape[1]
    fh = ff // 2
    b = fh // q_n

    def span(start, size, unit):
        return pl.ds(pl.multiple_of(start, unit), size)

    def rows(k):
        return span(k * slots, slots, 16)

    def mains(k, i):
        return span(k * slots + i * main, main, 16)

    def uppers(k):
        return span(k * slots, top, 16)

    def lowers(k):
        return span(k * slots + top, bottom, 16)

    def chunk_mains(k):
        return span(k * slots, nm, 16)

    def chunk_extras(k):
        return span(k * slots + nm, 16, 16)

    def places(e):
        return span(e * main, main, 16)

    def cols(k):
        return span(k * w, w, 128)

    def lanes(k):
        return span(k * 128, 128, 128)

    def tile(k):
        return span(k * 16, 16, 16)

    my_half = span(c * fh, fh, 128)
    other_half = span((1 - c) * fh, fh, 128)

    def block(qq):
        return span(c * fh + qq * b, b, 128)

    def copy(src, dst, send, recv, dp_at, ex_at):
        return pltpu.make_async_remote_copy(
            src_ref=src, dst_ref=dst, send_sem=send, recv_sem=recv,
            device_id=(dp_at, ex_at), device_id_type=pl.DeviceIdType.MESH,
        )

    def near(d):
        upper = (2 * z) // e_n
        low = z + upper * (e_n - 1 - 2 * z)
        side = 2 * lax.rem(d, 2) - 1
        at = jnp.where(d <= 2 * low, low + side * ((d + 1) // 2), d)
        return at + upper * (e_n - 1 - 2 * at)

    def back(d):
        return near(0 if d == 0 else e_n - d)

    def ways(i):
        to_left = on_x if i % 2 == 0 else 1 - on_x
        to_up = on_y if i // 2 == 0 else 1 - on_y
        return 2 * to_left + to_up, 2 * to_up + to_left

    def loop(lo, hi, body):
        def step(i, carry):
            body(i)
            return carry

        lax.fori_loop(lo, hi, step, 0)

    def partner(at, d, size):
        if size & (size - 1):
            return lax.rem(at + d, size)
        other, step = at, 1
        while step < size:
            if d & step:
                other = other + step - 2 * step * lax.rem(at // step, 2)
            step *= 2
        return other

    def to_plane(e, pairs):
        @pl.when(e != z)
        def _():
            for out, _ in pairs:
                out(m, e).start()

        @pl.when(e == z)
        def _():
            for _, own in pairs:
                own.start()

        for d in range(1, n):
            for out, _ in pairs:
                out(partner(m, d, n), e).start()

    def x_out(i, e):
        return copy(xs.at[places(e), cols(i)], xr.at[mains(z, m), :], sem_out.at[0], sem_in.at[0, z], i, e)

    x_own = pltpu.make_async_copy(xs.at[places(z), cols(m)], xr.at[mains(z, m), :], sem_in.at[0, z])

    def d_out(i, e):
        return copy(ds_.at[places(e), cols(i)], dr.at[mains(z, m), :], sem_out.at[1], sem_in.at[1, z], i, e)

    d_own = pltpu.make_async_copy(ds_.at[places(z), cols(m)], dr.at[mains(z, m), :], sem_in.at[1, z])

    def t_out(i, e):
        return copy(te.at[tile(e), lanes(i)], tiles.at[z, tile(m), :], sem_out.at[2], sem_in.at[2, z], i, e)

    t_own = pltpu.make_async_copy(te.at[tile(z), lanes(m)], tiles.at[z, tile(m), :], sem_in.at[2, z])

    def y_out(i, k):
        return copy(rs.at[mains(k, i), :], yb.at[places(z), cols(m)], sem_out.at[3], sem_back.at[0, m], i, k)

    y_own = pltpu.make_async_copy(rs.at[mains(z, m), :], yb.at[places(z), cols(m)], sem_back.at[0, m])

    def s_out(i, k):
        return copy(ss.at[mains(k, i), :], sb.at[places(z), cols(m)], sem_out.at[4], sem_back.at[1, m], i, k)

    s_own = pltpu.make_async_copy(ss.at[mains(z, m), :], sb.at[places(z), cols(m)], sem_back.at[1, m])

    def e_out_(i, k):
        return copy(et.at[tile(k * n + i), :], eb.at[tile(z), lanes(m)], sem_out.at[5], sem_ext.at[0], i, k)

    e_own = pltpu.make_async_copy(et.at[tile(z * n + m), :], eb.at[tile(z), lanes(m)], sem_ext.at[0])

    def arrived(ref, sem):
        copy(ref, ref, sem, sem, pm, z).wait_recv()

    def sent(ref, sem):
        copy(ref, ref, sem, sem, pm, z).wait_send()

    def pass_pair(no, src, dst):
        def out(k):
            return copy(src(k), dst(k), sem_ps.at[2 * no, k], sem_ps.at[2 * no + 1, k], pm, z)

        return out

    xf = pass_pair(0, lambda k: xr.at[rows(k)], lambda k: xp.at[rows(k)])
    df = pass_pair(1, lambda k: dr.at[rows(k)], lambda k: dp.at[rows(k)])

    def half_pass(no, ref):
        send, recv = sem_ps.at[2 * no], sem_ps.at[2 * no + 1]

        def out(k):
            part = ref.at[rows(k), my_half]
            return copy(part, part, send.at[k], recv.at[k], pm, z)

        def got(k):
            part = ref.at[rows(k), other_half]
            return copy(part, part, send.at[k], recv.at[k], pm, z)

        return out, got

    af_out, af_got = half_pass(2, act)
    ef_out, ef_got = half_pass(3, dga)
    uf_out, uf_got = half_pass(4, dua)

    def to_x(no, src, dst):
        return lambda k: copy(src(k), dst(k), sem_q.at[0, no, k], sem_q.at[1, no, k], mx, z)

    def to_y(no, src, dst):
        return lambda k: copy(src(k), dst(k), sem_q.at[0, no, k], sem_q.at[1, no, k], my, z)

    def same(no, to, part):
        return to(no, part, part)

    g1 = (
        to_x(0, lambda k: gs.at[k, 0, 2:4], lambda k: gr.at[k, 0]),
        to_y(1, lambda k: gs.at[k, 1, 2:4], lambda k: gr.at[k, 1]),
    )
    g2 = (
        to_y(2, lambda k: gs.at[k, 0, 1], lambda k: gt.at[k, 0]),
        to_x(3, lambda k: gs.at[k, 1, 1], lambda k: gt.at[k, 1]),
    )
    h1 = (
        to_x(4, lambda k: hst.at[k, 2:4], lambda k: hrt.at[k]),
        to_y(5, lambda k: hsb.at[k, 2:4], lambda k: hrb.at[k]),
    )
    h2 = (
        to_y(6, lambda k: hst.at[k, 1], lambda k: htt.at[k]),
        to_x(7, lambda k: hsb.at[k, 1], lambda k: htb.at[k]),
    )
    a1 = (
        same(8, to_x, lambda k: act.at[rows(k), block(q)]),
        same(9, to_y, lambda k: act.at[rows(k), block(q)]),
    )
    a2 = (
        same(10, to_y, lambda k: act.at[uppers(k), block(qx)]),
        same(11, to_x, lambda k: act.at[lowers(k), block(qy)]),
    )
    e1 = (
        same(12, to_x, lambda k: dga.at[rows(k), block(q)]),
        same(13, to_y, lambda k: dga.at[rows(k), block(q)]),
    )
    u1 = (
        same(14, to_x, lambda k: dua.at[rows(k), block(q)]),
        same(15, to_y, lambda k: dua.at[rows(k), block(q)]),
    )
    e2 = same(16, to_y, lambda k: dga.at[rows(k), block(qx)])
    u2 = same(17, to_x, lambda k: dua.at[rows(k), block(qy)])
    pw = [
        copy(wg_h.at[:, other_half], pwg, sem_pw.at[0, 0], sem_pw.at[1, 0], pm, z),
        copy(wu_h.at[:, other_half], pwu, sem_pw.at[0, 1], sem_pw.at[1, 1], pm, z),
        copy(wd_h.at[other_half], pwd, sem_pw.at[0, 2], sem_pw.at[1, 2], pm, z),
    ]
    own = [
        pltpu.make_async_copy(src, dst, sem_own.at[i])
        for i, (src, dst) in enumerate(((wg_h, wg), (wu_h, wu), (wd_h, wd)))
    ]
    for one in own:
        one.start()
    barrier = pltpu.get_barrier_semaphore()
    here = m * e_n + z

    def greet(d):
        other = lax.rem(here + d, n * e_n)
        pl.semaphore_signal(
            barrier, inc=1, device_id=(other // e_n, lax.rem(other, e_n)),
            device_id_type=pl.DeviceIdType.MESH,
        )

    loop(1, n * e_n, greet)

    name = route[...]
    share = prob[...].astype(F32)
    hits = jnp.where(lax.broadcasted_iota(jnp.int32, (16, t_rows), 0) == name, 1.0, 0.0)
    earlier = jnp.where(
        lax.broadcasted_iota(jnp.int32, (t_rows, t_rows), 0)
        < lax.broadcasted_iota(jnp.int32, (t_rows, t_rows), 1), 1.0, 0.0,
    ).astype(BF)
    place = jnp.sum(nn(hits.astype(BF), earlier) * hits, axis=0, keepdims=True).astype(jnp.int32)
    target = jnp.where(
        place < main, name * main + place, em + name * extra + place - main
    )
    hit = lax.broadcasted_iota(jnp.int32, (em + 16, t_rows), 0) == target
    tab[...] = jnp.where(hit, 1.0, 0.0).astype(BF)
    tabw[...] = jnp.where(hit, share, 0.0).astype(BF)

    def packing(count, flip):
        shape = (count * 16, 2 * cbs * 16) if flip else (2 * cbs * 16, count * 16)
        long = lax.broadcasted_iota(jnp.int32, shape, 1 if flip else 0)
        packed = lax.broadcasted_iota(jnp.int32, shape, 0 if flip else 1)
        slot = long & 15
        group = long >> 4
        want = ((slot >> flat_bits(extra)) << 4) + group * extra + (slot & (extra - 1))
        return jnp.where((packed == want) & (slot < count * extra), 1.0, 0.0).astype(BF)

    def gather(table, src, dst, a):
        for i in range(n):
            at = slice(i * w, (i + 1) * w)
            part = nn(table[...], src[:, at]).astype(BF)
            dst[:, at] = part[:em]
            for cb in range(cbs):
                g = (a * cbs + cb) * 16
                st[g:g + 16, i * 128:(i + 1) * 128] = part[em:, cb * 128:(cb + 1) * 128]

    gather(tab, tok, xs, 0)
    pl.semaphore_wait(barrier, n * e_n - 1)
    to_plane(z, [(x_out, x_own)])
    gather(tabw, cot, ds_, 1)
    pet[...] = packing(e_n, True)
    te[...] = nn(pet[...], st[...]).astype(BF)
    to_plane(z, [(t_out, t_own)])
    loop(1, e_n, lambda d: to_plane(near(d), [(x_out, x_own), (t_out, t_own)]))
    for one in pw:
        one.start()
    pn[...] = packing(n, False)
    pnt[...] = packing(n, True)
    pe[...] = packing(e_n, False)
    for one in own:
        one.wait()
    for one in pw:
        one.wait_recv()

    def x_in(k):
        arrived(tiles.at[k], sem_in.at[2, k])
        spare = nn(pn[...], tiles[k]).astype(BF)
        for cb in range(cbs):
            at = slice(cb * 128, (cb + 1) * 128)
            xr[chunk_extras(k), at] = spare[cb * 16:(cb + 1) * 16]
            dr[chunk_extras(k), at] = spare[(cbs + cb) * 16:(cbs + cb + 1) * 16]
        arrived(xr.at[chunk_mains(k)], sem_in.at[0, k])
        xf(k).start()

    def gate_up(k):
        mine = [nn(xr[rows(k), :], own_w[:, my_half]) for own_w in (wg, wu)]
        xf(k).wait_recv()
        for at, other_w in ((0, pwg), (1, pwu)):
            part = (mine[at] + nn(xp[rows(k), :], other_w[...])).astype(BF)
            for i in range(q_n):
                gs[k, at, ways(i)[at]] = part[:, i * b:(i + 1) * b]
            g1[at](k).start()

    def gate_mid(k):
        for at, keep in ((0, pre), (1, upv)):
            g1[at](k).wait_recv()
            gs[k, at, 1] = (gs[k, at, 1].astype(F32) + gr[k, at, 1].astype(F32)).astype(BF)
            g2[at](k).start()
            keep[rows(k), :] = gs[k, at, 0].astype(F32) + gr[k, at, 0].astype(F32)

    def dout_send(k):
        to_plane(k, [(d_out, d_own)])

    def activate(k):
        for one in g2:
            one(k).wait_recv()
        gate = pre[rows(k), :] + gt[k, 0].astype(F32)
        up = upv[rows(k), :] + gt[k, 1].astype(F32)
        act[rows(k), block(q)] = (gate * jax.nn.sigmoid(gate) * up).astype(BF)
        for one in a1:
            one(k).start()
        pre[rows(k), :] = gate
        upv[rows(k), :] = up

    def act_on(k):
        for near_one, on in zip(a1, a2):
            near_one(k).wait_recv()
            on(k).start()

    def act_pass(k):
        for one in a2:
            one(k).wait_recv()
        af_out(k).start()

    def result_rows(k):
        af_got(k).wait_recv()
        rs[rows(k), :] = nn(act[rows(k), :], wd[...]).astype(BF)
        to_plane(k, [(y_out, y_own)])

    def d_in(k):
        arrived(dr.at[chunk_mains(k)], sem_in.at[1, k])
        df(k).start()

    def down(k):
        mine = nt(dr[rows(k), :], wd[my_half, :])
        df(k).wait_recv()
        part = (mine + nt(dp[rows(k), :], pwd[...])).astype(BF)
        for i in range(q_n):
            at = slice(i * b, (i + 1) * b)
            hst[k, ways(i)[0]] = part[:top, at]
            hsb[k, ways(i)[1]] = part[top:, at]
        for one in h1:
            one(k).start()

    def down_mid(k):
        for first, then, had, got, place in ((h1[0], h2[0], hst, hrt, uppers), (h1[1], h2[1], hsb, hrb, lowers)):
            first(k).wait_recv()
            had[k, 1] = (had[k, 1].astype(F32) + got[k, 1].astype(F32)).astype(BF)
            then(k).start()
            dsum[place(k), :] = had[k, 0].astype(F32) + got[k, 0].astype(F32)

    def act_grad(k):
        for then, got, place in ((h2[0], htt, uppers), (h2[1], htb, lowers)):
            then(k).wait_recv()
            total = dsum[place(k), :] + got[k].astype(F32)
            gate, up = pre[place(k), :], upv[place(k), :]
            sig = jax.nn.sigmoid(gate)
            dga[place(k), block(q)] = (total * up * sig * (1.0 + gate * (1.0 - sig))).astype(BF)
            dua[place(k), block(q)] = (total * gate * sig).astype(BF)
        for one in (*e1, *u1):
            one(k).start()

    def grad_on(k):
        e1[0](k).wait_recv()
        e2(k).start()
        u1[1](k).wait_recv()
        u2(k).start()

    def handed(k):
        e1[1](k).wait_recv()
        e2(k).wait_recv()
        ef_out(k).start()
        u1[0](k).wait_recv()
        u2(k).wait_recv()
        uf_out(k).start()

    def input_grad(k):
        ef_got(k).wait_recv()
        uf_got(k).wait_recv()
        ss[rows(k), :] = (nt(dga[rows(k), :], wg[...]) + nt(dua[rows(k), :], wu[...])).astype(BF)
        to_plane(k, [(s_out, s_own)])
        long = [
            buf[chunk_extras(k), cb * 128:(cb + 1) * 128] for buf in (rs, ss) for cb in range(cbs)
        ]
        et[span(k * n * 16, n * 16, 16), :] = nn(pnt[...], jnp.concatenate(long, axis=0)).astype(BF)
        to_plane(k, [(e_out_, e_own)])

    ahead = (
        (gate_mid, 1, 0), (x_in, 0, 1), (act_on, 2, 2), (gate_up, 0, 4),
        (activate, 1, 7), (act_pass, 2, 8), (result_rows, 3, 10),
    )
    behind = (
        (down_mid, 3, 3), (d_in, 2, 6), (grad_on, 4, 9), (down, 2, 11), (act_grad, 3, 12), (handed, 4, 13), (input_grad, 5, 14),
    )
    plan = []
    for d in range(e_n):
        plan += [(d + lag, at, body, near(d)) for body, lag, at in ahead]
        plan += [(lag + (d and d + 1), at, body, back(d)) for body, lag, at in behind]
        plan += [(d and min(d + 1, e_n - 1), 5 + d / 100, dout_send, back(d))]
    for _, _, body, k in sorted(plan, key=lambda one: one[:2]):
        body(k)

    x_t[...] = xr[...].T
    wide = 2 * b

    def down_grad(j):
        at = span(j * wide, wide, 128)
        gd_o[at, :] = tn(act[:, at], dr[...]).astype(BF)

    loop(0, ff // wide, down_grad)

    def weight_grad(j):
        at = span(j * wide, wide, 128)
        gg_o[:, at] = nn(x_t[...], dga[:, at]).astype(BF)
        gu_o[:, at] = nn(x_t[...], dua[:, at]).astype(BF)

    loop(0, ff // wide, weight_grad)

    arrived(eb, sem_ext.at[0])
    spare = nn(pe[...], eb[...]).astype(BF)
    for a, buf in ((0, yb), (1, sb)):
        for cb in range(cbs):
            g = (a * cbs + cb) * 16
            for i in range(n):
                buf[em:em + 16, i * w + cb * 128:i * w + (cb + 1) * 128] = spare[g:g + 16, i * 128:(i + 1) * 128]

    def combine(a, table, buf, out):
        def one(i):
            arrived(buf.at[0:em, cols(i)], sem_back.at[a, i])
            out[:, cols(i)] = tn(table[...], buf[:, cols(i)]).astype(BF)

        loop(0, n, one)

    combine(0, tabw, yb, mix_o)
    combine(1, tab, sb, ig_o)

    for at in (0, 1, 3, 4):
        sent(xr.at[0:(n * e_n - 1) * main], sem_out.at[at])
    for at in (2, 5):
        sent(et.at[0:(n * e_n - 1) * 16], sem_out.at[at])
    for one in pw:
        one.wait_send()

    def chunk_end(k):
        for out in (xf, df, af_out, ef_out, uf_out):
            out(k).wait_send()
        for out in (*g1, *g2, *h1, *h2, *a1, *a2, *e1, *u1, e2, u2):
            out(k).wait_send()

    loop(0, e_n, chunk_end)


def fused_layer(tokens, probs, routes, w_gate, w_up, w_down, cotangent, n, e_n, cap):
    t_rows, width = tokens.shape
    w = width // n
    ff = w_gate.shape[2]
    slots, fh, q_n = n * cap, ff // 2, n // 2
    b = fh // q_n
    r = e_n * slots
    main = cap // 16 * 16
    top = (slots // 16 + 1) // 2 * 16
    bottom = slots - top
    tr, cbs = e_n * main + 16, w // 128
    long = 2 * cbs * 16
    vm = pl.BlockSpec(memory_space=pltpu.VMEM)

    def v(*shape, dtype=BF):
        return pltpu.VMEM(shape, dtype)

    scratch = [
        v(tr, t_rows), v(tr, t_rows), v(long, n * 16), v(n * 16, long), v(long, e_n * 16), v(e_n * 16, long),
        v(long, n * 128), v(e_n * 16, n * 128), v(e_n, n * 16, 128), v(e_n * n * 16, 128), v(e_n * 16, n * 128),
        v(e_n * main, width), v(e_n * main, width),
        v(r, w), v(r, w), v(r, w), v(r, w),
        v(w, fh), v(w, fh), v(fh, w),
        v(e_n, 2, q_n, slots, b), v(e_n, 2, 2, slots, b), v(e_n, 2, slots, b),
        v(e_n, q_n, top, b), v(e_n, q_n, bottom, b), v(e_n, 2, top, b), v(e_n, 2, bottom, b),
        v(e_n, top, b), v(e_n, bottom, b),
        v(r, b, dtype=F32), v(r, b, dtype=F32), v(r, b, dtype=F32),
        v(r, ff), v(r, ff), v(r, ff),
        v(r, w), v(r, w), v(tr, width), v(tr, width),
        v(w, r), v(w, ff), v(w, ff), v(ff, w),
        pltpu.SemaphoreType.DMA((3,)),
        pltpu.SemaphoreType.DMA((2, 3)),
        pltpu.SemaphoreType.DMA((6,)),
        pltpu.SemaphoreType.DMA((3, e_n)),
        pltpu.SemaphoreType.DMA((2, n)),
        pltpu.SemaphoreType.DMA((1,)),
        pltpu.SemaphoreType.DMA((10, e_n)),
        pltpu.SemaphoreType.DMA((2, 18, e_n)),
    ]
    mixed, input_grad, gg, gu, gd = pl.pallas_call(
        functools.partial(layer_kernel, n, e_n, cap),
        out_shape=(
            jax.ShapeDtypeStruct((t_rows, width), BF),
            jax.ShapeDtypeStruct((t_rows, width), BF),
            jax.ShapeDtypeStruct((w, ff), BF),
            jax.ShapeDtypeStruct((w, ff), BF),
            jax.ShapeDtypeStruct((ff, w), BF),
        ),
        in_specs=[vm] * 4 + [pl.BlockSpec(memory_space=pl.ANY)] * 3,
        out_specs=(vm,) * 5,
        scratch_shapes=scratch,
        compiler_params=pltpu.CompilerParams(
            collective_id=0, has_side_effects=True, vmem_limit_bytes=62 * 1024 * 1024
        ),
    )(tokens, cotangent, routes.reshape(1, -1), probs.reshape(1, -1), w_gate[0], w_up[0], w_down[0])
    return mixed, input_grad, gg[None], gu[None], gd[None]


def packs(n, e_n, cap, width):
    extra, cbs = cap % 16, width // n // 128
    return (
        n == 8 and cap > 16 and extra > 0 and extra & (extra - 1) == 0 and n & (n - 1) == 0
        and n * extra == 16 and e_n * extra <= 16 and 2 * extra * cbs == 16
    )


def slot_table(routes, experts_all, capacity):
    flat = routes.reshape(-1)
    hits = (flat[:, None] == jnp.arange(experts_all, dtype=jnp.int32)[None, :]).astype(jnp.int32)
    at = jnp.arange(flat.shape[0], dtype=jnp.int32)
    earlier = (at[:, None] > at[None, :]).astype(BF)
    before = nn(earlier, hits.astype(BF)).astype(jnp.int32)
    place = jnp.sum(before * hits, axis=1)
    target = flat * capacity + place
    table = jnp.arange(experts_all * capacity, dtype=jnp.int32)[:, None] == target[None, :]
    return table.astype(jnp.bfloat16)


def spread_rows(table, values, slices):
    shaped = values.reshape(values.shape[0], slices, values.shape[1] // slices)
    return jnp.einsum("st,tnk->nsk", table, shaped, preferred_element_type=jnp.float32).astype(
        jnp.bfloat16
    )


def to_rows(received, local_count):
    sources, slots, width = received.shape
    shaped = received.reshape(sources, local_count, slots // local_count, width)
    shaped = jnp.swapaxes(shaped, 1, 2)
    return shaped.reshape(sources * (slots // local_count), local_count, width)


def to_sources(rowwise, capacity):
    total, local_count, width = rowwise.shape
    shaped = rowwise.reshape(total // capacity, capacity, local_count, width)
    shaped = jnp.swapaxes(shaped, 1, 2)
    return shaped.reshape(total // capacity, local_count * capacity, width)


def collect(table, back, tok_rows, top):
    picked = jnp.einsum("st,nsk->tnk", table, back, preferred_element_type=jnp.float32)
    return picked.reshape(tok_rows, top, -1)


def per_device(tokens, probs, routes, w_gate, w_up, w_down, cotangent):
    local_count = w_gate.shape[0]
    n_dp = lax.axis_size("dp")
    n_exp = lax.axis_size("expert")
    experts_all = local_count * n_exp
    tok_rows, width = tokens.shape
    top = routes.shape[1]
    capacity = max(2, 17 * tok_rows * top // (16 * experts_all))
    ff = w_gate.shape[2]
    if (
        local_count == 1 and top == 1 and n_dp % 2 == 0 and ff % (n_dp * 128) == 0
        and tok_rows % 128 == 0 and width % (n_dp * 128) == 0 and packs(n_dp, n_exp, capacity, width)
    ):
        return fused_layer(
            tokens, probs, routes, w_gate, w_up, w_down, cotangent, n_dp, n_exp, capacity
        )
    blocks = n_dp * n_exp
    slot_width = width // n_dp
    table = slot_table(routes, experts_all, capacity)
    x_send = spread_rows(table, jnp.repeat(tokens, top, axis=0), n_dp)
    x_send = x_send.reshape(blocks, local_count * capacity, slot_width)
    weight = probs.astype(jnp.float32)
    scaled = (jnp.repeat(cotangent, top, axis=0).astype(jnp.float32) * weight).astype(jnp.bfloat16)
    x_got = lax.all_to_all(x_send, ("dp", "expert"), split_axis=0, concat_axis=0, tiled=True)
    rows = to_rows(x_got, local_count)
    part = rows
    gate = jnp.einsum("red,edf->ref", part, w_gate, preferred_element_type=jnp.float32)
    upper = jnp.einsum("red,edf->ref", part, w_up, preferred_element_type=jnp.float32)
    summed = lax.psum_scatter(
        jnp.stack([gate, upper], axis=2).astype(jnp.bfloat16), "dp", scatter_dimension=0, tiled=True
    ).astype(jnp.float32)
    gate_pre = summed[:, :, 0]
    up_value = summed[:, :, 1]
    sig = jax.nn.sigmoid(gate_pre)
    act = (gate_pre * sig * up_value).astype(jnp.bfloat16)
    act_all = lax.all_gather(act, "dp", axis=0, tiled=True)
    result = jnp.einsum("ref,efd->red", act_all, w_down, preferred_element_type=jnp.float32).astype(
        jnp.bfloat16
    )
    outgoing = to_sources(result, capacity)
    back = lax.all_to_all(outgoing, ("dp", "expert"), split_axis=0, concat_axis=0, tiled=True)
    back = back.reshape(n_dp, experts_all * capacity, slot_width)
    picked = collect(table, back, tok_rows, top)
    mixed = jnp.sum(picked * weight[..., None], axis=1).astype(jnp.bfloat16)
    dy_send = spread_rows(table, scaled, n_dp).reshape(blocks, local_count * capacity, slot_width)
    dy_got = lax.all_to_all(dy_send, ("dp", "expert"), split_axis=0, concat_axis=0, tiled=True)
    dout = to_rows(dy_got, local_count)
    grad_down = jnp.einsum("ref,red->efd", act_all, dout, preferred_element_type=jnp.float32)
    part = dout
    dact = lax.psum_scatter(
        jnp.einsum("red,efd->ref", part, w_down, preferred_element_type=jnp.float32).astype(
            jnp.bfloat16
        ),
        "dp",
        scatter_dimension=0,
        tiled=True,
    ).astype(jnp.float32)
    dgate = (dact * up_value * sig * (1.0 + gate_pre * (1.0 - sig))).astype(jnp.bfloat16)
    dup = (dact * gate_pre * sig).astype(jnp.bfloat16)
    dgate_all, dup_all = (
        lax.all_gather(dgate, "dp", axis=0, tiled=True),
        lax.all_gather(dup, "dp", axis=0, tiled=True),
    )
    grad_gate = jnp.einsum("red,ref->edf", rows, dgate_all, preferred_element_type=jnp.float32)
    grad_up = jnp.einsum("red,ref->edf", rows, dup_all, preferred_element_type=jnp.float32)
    slot_grad = jnp.einsum(
        "ref,edf->red", dgate_all, w_gate, preferred_element_type=jnp.float32
    ) + jnp.einsum("ref,edf->red", dup_all, w_up, preferred_element_type=jnp.float32)
    slot_grad = slot_grad.astype(jnp.bfloat16)
    returned = lax.all_to_all(
        to_sources(slot_grad, capacity), ("dp", "expert"), split_axis=0, concat_axis=0, tiled=True
    )
    returned = returned.reshape(n_dp, experts_all * capacity, slot_width)
    input_grad = jnp.sum(collect(table, returned, tok_rows, top), axis=1).astype(jnp.bfloat16)
    return (
        mixed,
        input_grad,
        grad_gate.astype(jnp.bfloat16),
        grad_up.astype(jnp.bfloat16),
        grad_down.astype(jnp.bfloat16),
    )


def solution(mesh):
    return jax.shard_map(
        per_device,
        mesh=mesh,
        in_specs=(
            P(("dp", "expert"), None),
            P(("dp", "expert"), None),
            P(("dp", "expert"), None),
            P("expert", "dp", None),
            P("expert", "dp", None),
            P("expert", None, "dp"),
            P(("dp", "expert"), None),
        ),
        out_specs=(
            P(("dp", "expert"), None),
            P(("dp", "expert"), None),
            P("expert", "dp", None),
            P("expert", "dp", None),
            P("expert", None, "dp"),
        ),
        check_vma=False,
    )
```

```python
import functools

import jax
import jax.numpy as jnp
from jax import lax
from jax.experimental import pallas as pl
from jax.experimental.pallas import tpu as pltpu
from jax.sharding import PartitionSpec as P

BF = jnp.bfloat16
F32 = jnp.float32


def nn(a, b):
    return lax.dot_general(a, b, (((1,), (0,)), ((), ())), preferred_element_type=F32)


def nt(a, b):
    return lax.dot_general(a, b, (((1,), (1,)), ((), ())), preferred_element_type=F32)


def tn(a, b):
    return lax.dot_general(a, b, (((0,), (0,)), ((), ())), preferred_element_type=F32)


def flat_bits(value):
    return value.bit_length() - 1


def layer_kernel(
    n, e_n, cap,
    tok, cot, route, prob, wg_h, wu_h, wd_h,
    mix_o, ig_o, gg_o, gu_o, gd_o,
    tab, tabw, pn, pnt, pe, pet, st, te, tiles, et, eb,
    xs, ds_, xr, dr, xp, dp, pwg, pwu, pwd,
    gs, gr, gt, hst, hsb, hrt, hrb, htt, htb, dsum, pre, upv, act, dga, dua, rs, ss, yb, sb, x_t, wg, wu, wd,
    sem_own, sem_pw, sem_out, sem_in, sem_back, sem_ext, sem_ps, sem_q,
):
    m = lax.axis_index("dp")
    z = lax.axis_index("expert")
    q_n = n // 2
    q = m // 2
    c = lax.rem(m, 2)
    pm = m + 1 - 2 * c
    on_x, on_y = lax.rem(q, 2), q // 2
    qx, qy = q + 1 - 2 * on_x, q + 2 - 4 * on_y
    mx, my = 2 * qx + c, 2 * qy + c
    slots = n * cap
    top = (slots // 16 + 1) // 2 * 16
    bottom = slots - top
    main = cap // 16 * 16
    extra = cap - main
    em, nm = e_n * main, n * main
    t_rows, w = tok.shape[0], tok.shape[1] // n
    cbs = w // 128
    ff = wg_h.shape[1]
    fh = ff // 2
    b = fh // q_n

    def span(start, size, unit):
        return pl.ds(pl.multiple_of(start, unit), size)

    def rows(k):
        return span(k * slots, slots, 16)

    def mains(k, i):
        return span(k * slots + i * main, main, 16)

    def uppers(k):
        return span(k * slots, top, 16)

    def lowers(k):
        return span(k * slots + top, bottom, 16)

    def chunk_mains(k):
        return span(k * slots, nm, 16)

    def chunk_extras(k):
        return span(k * slots + nm, 16, 16)

    def places(e):
        return span(e * main, main, 16)

    def cols(k):
        return span(k * w, w, 128)

    def lanes(k):
        return span(k * 128, 128, 128)

    def tile(k):
        return span(k * 16, 16, 16)

    my_half = span(c * fh, fh, 128)
    other_half = span((1 - c) * fh, fh, 128)

    def block(qq):
        return span(c * fh + qq * b, b, 128)

    def copy(src, dst, send, recv, dp_at, ex_at):
        return pltpu.make_async_remote_copy(
            src_ref=src, dst_ref=dst, send_sem=send, recv_sem=recv,
            device_id=(dp_at, ex_at), device_id_type=pl.DeviceIdType.MESH,
        )

    def near(d):
        upper = (2 * z) // e_n
        low = z + upper * (e_n - 1 - 2 * z)
        side = 2 * lax.rem(d, 2) - 1
        at = jnp.where(d <= 2 * low, low + side * ((d + 1) // 2), d)
        return at + upper * (e_n - 1 - 2 * at)

    def back(d):
        return near(0 if d == 0 else e_n - d)

    def ways(i):
        to_left = on_x if i % 2 == 0 else 1 - on_x
        to_up = on_y if i // 2 == 0 else 1 - on_y
        return 2 * to_left + to_up, 2 * to_up + to_left

    def loop(lo, hi, body):
        def step(i, carry):
            body(i)
            return carry

        lax.fori_loop(lo, hi, step, 0)

    def partner(at, d, size):
        if size & (size - 1):
            return lax.rem(at + d, size)
        other, step = at, 1
        while step < size:
            if d & step:
                other = other + step - 2 * step * lax.rem(at // step, 2)
            step *= 2
        return other

    def to_plane(e, pairs):
        @pl.when(e != z)
        def _():
            for out, _ in pairs:
                out(m, e).start()

        @pl.when(e == z)
        def _():
            for _, own in pairs:
                own.start()

        for d in range(1, n):
            for out, _ in pairs:
                out(partner(m, d, n), e).start()

    def x_out(i, e):
        return copy(xs.at[places(e), cols(i)], xr.at[mains(z, m), :], sem_out.at[0], sem_in.at[0, z], i, e)

    x_own = pltpu.make_async_copy(xs.at[places(z), cols(m)], xr.at[mains(z, m), :], sem_in.at[0, z])

    def d_out(i, e):
        return copy(ds_.at[places(e), cols(i)], dr.at[mains(z, m), :], sem_out.at[1], sem_in.at[1, z], i, e)

    d_own = pltpu.make_async_copy(ds_.at[places(z), cols(m)], dr.at[mains(z, m), :], sem_in.at[1, z])

    def t_out(i, e):
        return copy(te.at[tile(e), lanes(i)], tiles.at[z, tile(m), :], sem_out.at[2], sem_in.at[2, z], i, e)

    t_own = pltpu.make_async_copy(te.at[tile(z), lanes(m)], tiles.at[z, tile(m), :], sem_in.at[2, z])

    def y_out(i, k):
        return copy(rs.at[mains(k, i), :], yb.at[places(z), cols(m)], sem_out.at[3], sem_back.at[0, m], i, k)

    y_own = pltpu.make_async_copy(rs.at[mains(z, m), :], yb.at[places(z), cols(m)], sem_back.at[0, m])

    def s_out(i, k):
        return copy(ss.at[mains(k, i), :], sb.at[places(z), cols(m)], sem_out.at[4], sem_back.at[1, m], i, k)

    s_own = pltpu.make_async_copy(ss.at[mains(z, m), :], sb.at[places(z), cols(m)], sem_back.at[1, m])

    def e_out_(i, k):
        return copy(et.at[tile(k * n + i), :], eb.at[tile(z), lanes(m)], sem_out.at[5], sem_ext.at[0], i, k)

    e_own = pltpu.make_async_copy(et.at[tile(z * n + m), :], eb.at[tile(z), lanes(m)], sem_ext.at[0])

    def arrived(ref, sem):
        copy(ref, ref, sem, sem, pm, z).wait_recv()

    def sent(ref, sem):
        copy(ref, ref, sem, sem, pm, z).wait_send()

    def pass_pair(no, src, dst):
        def out(k):
            return copy(src(k), dst(k), sem_ps.at[2 * no, k], sem_ps.at[2 * no + 1, k], pm, z)

        return out

    xf = pass_pair(0, lambda k: xr.at[rows(k)], lambda k: xp.at[rows(k)])
    df = pass_pair(1, lambda k: dr.at[rows(k)], lambda k: dp.at[rows(k)])

    def half_pass(no, ref):
        send, recv = sem_ps.at[2 * no], sem_ps.at[2 * no + 1]

        def out(k):
            part = ref.at[rows(k), my_half]
            return copy(part, part, send.at[k], recv.at[k], pm, z)

        def got(k):
            part = ref.at[rows(k), other_half]
            return copy(part, part, send.at[k], recv.at[k], pm, z)

        return out, got

    af_out, af_got = half_pass(2, act)
    ef_out, ef_got = half_pass(3, dga)
    uf_out, uf_got = half_pass(4, dua)

    def to_x(no, src, dst):
        return lambda k: copy(src(k), dst(k), sem_q.at[0, no, k], sem_q.at[1, no, k], mx, z)

    def to_y(no, src, dst):
        return lambda k: copy(src(k), dst(k), sem_q.at[0, no, k], sem_q.at[1, no, k], my, z)

    def same(no, to, part):
        return to(no, part, part)

    g1 = (
        to_x(0, lambda k: gs.at[k, 0, 2:4], lambda k: gr.at[k, 0]),
        to_y(1, lambda k: gs.at[k, 1, 2:4], lambda k: gr.at[k, 1]),
    )
    g2 = (
        to_y(2, lambda k: gs.at[k, 0, 1], lambda k: gt.at[k, 0]),
        to_x(3, lambda k: gs.at[k, 1, 1], lambda k: gt.at[k, 1]),
    )
    h1 = (
        to_x(4, lambda k: hst.at[k, 2:4], lambda k: hrt.at[k]),
        to_y(5, lambda k: hsb.at[k, 2:4], lambda k: hrb.at[k]),
    )
    h2 = (
        to_y(6, lambda k: hst.at[k, 1], lambda k: htt.at[k]),
        to_x(7, lambda k: hsb.at[k, 1], lambda k: htb.at[k]),
    )
    a1 = (
        same(8, to_x, lambda k: act.at[rows(k), block(q)]),
        same(9, to_y, lambda k: act.at[rows(k), block(q)]),
    )
    a2 = (
        same(10, to_y, lambda k: act.at[uppers(k), block(qx)]),
        same(11, to_x, lambda k: act.at[lowers(k), block(qy)]),
    )
    e1 = (
        same(12, to_x, lambda k: dga.at[rows(k), block(q)]),
        same(13, to_y, lambda k: dga.at[rows(k), block(q)]),
    )
    u1 = (
        same(14, to_x, lambda k: dua.at[rows(k), block(q)]),
        same(15, to_y, lambda k: dua.at[rows(k), block(q)]),
    )
    e2 = same(16, to_y, lambda k: dga.at[rows(k), block(qx)])
    u2 = same(17, to_x, lambda k: dua.at[rows(k), block(qy)])
    pw = [
        copy(wg_h.at[:, other_half], pwg, sem_pw.at[0, 0], sem_pw.at[1, 0], pm, z),
        copy(wu_h.at[:, other_half], pwu, sem_pw.at[0, 1], sem_pw.at[1, 1], pm, z),
        copy(wd_h.at[other_half], pwd, sem_pw.at[0, 2], sem_pw.at[1, 2], pm, z),
    ]
    own = [
        pltpu.make_async_copy(src, dst, sem_own.at[i])
        for i, (src, dst) in enumerate(((wg_h, wg), (wu_h, wu), (wd_h, wd)))
    ]
    for one in own:
        one.start()
    barrier = pltpu.get_barrier_semaphore()
    here = m * e_n + z

    def greet(d):
        other = lax.rem(here + d, n * e_n)
        pl.semaphore_signal(
            barrier, inc=1, device_id=(other // e_n, lax.rem(other, e_n)),
            device_id_type=pl.DeviceIdType.MESH,
        )

    loop(1, n * e_n, greet)

    name = route[...]
    share = prob[...].astype(F32)
    hits = jnp.where(lax.broadcasted_iota(jnp.int32, (16, t_rows), 0) == name, 1.0, 0.0)
    earlier = jnp.where(
        lax.broadcasted_iota(jnp.int32, (t_rows, t_rows), 0)
        < lax.broadcasted_iota(jnp.int32, (t_rows, t_rows), 1), 1.0, 0.0,
    ).astype(BF)
    place = jnp.sum(nn(hits.astype(BF), earlier) * hits, axis=0, keepdims=True).astype(jnp.int32)
    target = jnp.where(
        place < main, name * main + place, em + name * extra + place - main
    )
    hit = lax.broadcasted_iota(jnp.int32, (em + 16, t_rows), 0) == target
    tab[...] = jnp.where(hit, 1.0, 0.0).astype(BF)
    tabw[...] = jnp.where(hit, share, 0.0).astype(BF)

    def packing(count, flip):
        shape = (count * 16, 2 * cbs * 16) if flip else (2 * cbs * 16, count * 16)
        long = lax.broadcasted_iota(jnp.int32, shape, 1 if flip else 0)
        packed = lax.broadcasted_iota(jnp.int32, shape, 0 if flip else 1)
        slot = long & 15
        group = long >> 4
        want = ((slot >> flat_bits(extra)) << 4) + group * extra + (slot & (extra - 1))
        return jnp.where((packed == want) & (slot < count * extra), 1.0, 0.0).astype(BF)

    def gather(table, src, dst, a):
        for i in range(n):
            at = slice(i * w, (i + 1) * w)
            part = nn(table[...], src[:, at]).astype(BF)
            dst[:, at] = part[:em]
            for cb in range(cbs):
                g = (a * cbs + cb) * 16
                st[g:g + 16, i * 128:(i + 1) * 128] = part[em:, cb * 128:(cb + 1) * 128]

    gather(tab, tok, xs, 0)
    pl.semaphore_wait(barrier, n * e_n - 1)
    to_plane(z, [(x_out, x_own)])
    gather(tabw, cot, ds_, 1)
    pet[...] = packing(e_n, True)
    te[...] = nn(pet[...], st[...]).astype(BF)
    to_plane(z, [(t_out, t_own)])
    loop(1, e_n, lambda d: to_plane(near(d), [(x_out, x_own), (t_out, t_own)]))
    for one in pw:
        one.start()
    pn[...] = packing(n, False)
    pnt[...] = packing(n, True)
    pe[...] = packing(e_n, False)
    for one in own:
        one.wait()
    for one in pw:
        one.wait_recv()

    def x_in(k):
        arrived(tiles.at[k], sem_in.at[2, k])
        spare = nn(pn[...], tiles[k]).astype(BF)
        for cb in range(cbs):
            at = slice(cb * 128, (cb + 1) * 128)
            xr[chunk_extras(k), at] = spare[cb * 16:(cb + 1) * 16]
            dr[chunk_extras(k), at] = spare[(cbs + cb) * 16:(cbs + cb + 1) * 16]
        arrived(xr.at[chunk_mains(k)], sem_in.at[0, k])
        xf(k).start()

    def gate_up(k):
        mine = [nn(xr[rows(k), :], own_w[:, my_half]) for own_w in (wg, wu)]
        xf(k).wait_recv()
        for at, other_w in ((0, pwg), (1, pwu)):
            part = (mine[at] + nn(xp[rows(k), :], other_w[...])).astype(BF)
            for i in range(q_n):
                gs[k, at, ways(i)[at]] = part[:, i * b:(i + 1) * b]
            g1[at](k).start()

    def gate_mid(k):
        for at, keep in ((0, pre), (1, upv)):
            g1[at](k).wait_recv()
            gs[k, at, 1] = (gs[k, at, 1].astype(F32) + gr[k, at, 1].astype(F32)).astype(BF)
            g2[at](k).start()
            keep[rows(k), :] = gs[k, at, 0].astype(F32) + gr[k, at, 0].astype(F32)

    def dout_send(k):
        to_plane(k, [(d_out, d_own)])

    def activate(k):
        for one in g2:
            one(k).wait_recv()
        gate = pre[rows(k), :] + gt[k, 0].astype(F32)
        up = upv[rows(k), :] + gt[k, 1].astype(F32)
        act[rows(k), block(q)] = (gate * jax.nn.sigmoid(gate) * up).astype(BF)
        for one in a1:
            one(k).start()
        pre[rows(k), :] = gate
        upv[rows(k), :] = up

    def act_on(k):
        for near_one, on in zip(a1, a2):
            near_one(k).wait_recv()
            on(k).start()

    def act_pass(k):
        for one in a2:
            one(k).wait_recv()
        af_out(k).start()

    def result_rows(k):
        af_got(k).wait_recv()
        rs[rows(k), :] = nn(act[rows(k), :], wd[...]).astype(BF)
        to_plane(k, [(y_out, y_own)])

    def d_in(k):
        arrived(dr.at[chunk_mains(k)], sem_in.at[1, k])
        df(k).start()

    def down(k):
        mine = nt(dr[rows(k), :], wd[my_half, :])
        df(k).wait_recv()
        part = (mine + nt(dp[rows(k), :], pwd[...])).astype(BF)
        for i in range(q_n):
            at = slice(i * b, (i + 1) * b)
            hst[k, ways(i)[0]] = part[:top, at]
            hsb[k, ways(i)[1]] = part[top:, at]
        for one in h1:
            one(k).start()

    def down_mid(k):
        for first, then, had, got, place in ((h1[0], h2[0], hst, hrt, uppers), (h1[1], h2[1], hsb, hrb, lowers)):
            first(k).wait_recv()
            had[k, 1] = (had[k, 1].astype(F32) + got[k, 1].astype(F32)).astype(BF)
            then(k).start()
            dsum[place(k), :] = had[k, 0].astype(F32) + got[k, 0].astype(F32)

    def act_grad(k):
        for then, got, place in ((h2[0], htt, uppers), (h2[1], htb, lowers)):
            then(k).wait_recv()
            total = dsum[place(k), :] + got[k].astype(F32)
            gate, up = pre[place(k), :], upv[place(k), :]
            sig = jax.nn.sigmoid(gate)
            dga[place(k), block(q)] = (total * up * sig * (1.0 + gate * (1.0 - sig))).astype(BF)
            dua[place(k), block(q)] = (total * gate * sig).astype(BF)
        for one in (*e1, *u1):
            one(k).start()

    def grad_on(k):
        e1[0](k).wait_recv()
        e2(k).start()
        u1[1](k).wait_recv()
        u2(k).start()

    def handed(k):
        e1[1](k).wait_recv()
        e2(k).wait_recv()
        ef_out(k).start()
        u1[0](k).wait_recv()
        u2(k).wait_recv()
        uf_out(k).start()

    def input_grad(k):
        ef_got(k).wait_recv()
        uf_got(k).wait_recv()
        ss[rows(k), :] = (nt(dga[rows(k), :], wg[...]) + nt(dua[rows(k), :], wu[...])).astype(BF)
        to_plane(k, [(s_out, s_own)])
        long = [
            buf[chunk_extras(k), cb * 128:(cb + 1) * 128] for buf in (rs, ss) for cb in range(cbs)
        ]
        et[span(k * n * 16, n * 16, 16), :] = nn(pnt[...], jnp.concatenate(long, axis=0)).astype(BF)
        to_plane(k, [(e_out_, e_own)])

    ahead = (
        (gate_mid, 1, 0), (x_in, 0, 1), (act_on, 2, 2), (gate_up, 0, 4),
        (activate, 1, 7), (act_pass, 2, 8), (result_rows, 3, 10),
    )
    behind = (
        (down_mid, 3, 3), (d_in, 2, 6), (grad_on, 4, 9), (down, 2, 11), (act_grad, 3, 12), (handed, 4, 13), (input_grad, 5, 14),
    )
    plan = []
    for d in range(e_n):
        plan += [(d + lag, at, body, near(d)) for body, lag, at in ahead]
        plan += [(lag + (d and d + 1), at, body, back(d)) for body, lag, at in behind]
        plan += [(d and e_n - 1, 5 + d / 100, dout_send, back(d))]
    for _, _, body, k in sorted(plan, key=lambda one: one[:2]):
        body(k)

    x_t[...] = xr[...].T
    wide = 2 * b

    def down_grad(j):
        at = span(j * wide, wide, 128)
        gd_o[at, :] = tn(act[:, at], dr[...]).astype(BF)

    loop(0, ff // wide, down_grad)

    def weight_grad(j):
        at = span(j * wide, wide, 128)
        gg_o[:, at] = nn(x_t[...], dga[:, at]).astype(BF)
        gu_o[:, at] = nn(x_t[...], dua[:, at]).astype(BF)

    loop(0, ff // wide, weight_grad)

    arrived(eb, sem_ext.at[0])
    spare = nn(pe[...], eb[...]).astype(BF)
    for a, buf in ((0, yb), (1, sb)):
        for cb in range(cbs):
            g = (a * cbs + cb) * 16
            for i in range(n):
                buf[em:em + 16, i * w + cb * 128:i * w + (cb + 1) * 128] = spare[g:g + 16, i * 128:(i + 1) * 128]

    def combine(a, table, buf, out):
        def one(i):
            arrived(buf.at[0:em, cols(i)], sem_back.at[a, i])
            out[:, cols(i)] = tn(table[...], buf[:, cols(i)]).astype(BF)

        loop(0, n, one)

    combine(0, tabw, yb, mix_o)
    combine(1, tab, sb, ig_o)

    for at in (0, 1, 3, 4):
        sent(xr.at[0:(n * e_n - 1) * main], sem_out.at[at])
    for at in (2, 5):
        sent(et.at[0:(n * e_n - 1) * 16], sem_out.at[at])
    for one in pw:
        one.wait_send()

    def chunk_end(k):
        for out in (xf, df, af_out, ef_out, uf_out):
            out(k).wait_send()
        for out in (*g1, *g2, *h1, *h2, *a1, *a2, *e1, *u1, e2, u2):
            out(k).wait_send()

    loop(0, e_n, chunk_end)


def fused_layer(tokens, probs, routes, w_gate, w_up, w_down, cotangent, n, e_n, cap):
    t_rows, width = tokens.shape
    w = width // n
    ff = w_gate.shape[2]
    slots, fh, q_n = n * cap, ff // 2, n // 2
    b = fh // q_n
    r = e_n * slots
    main = cap // 16 * 16
    top = (slots // 16 + 1) // 2 * 16
    bottom = slots - top
    tr, cbs = e_n * main + 16, w // 128
    long = 2 * cbs * 16
    vm = pl.BlockSpec(memory_space=pltpu.VMEM)

    def v(*shape, dtype=BF):
        return pltpu.VMEM(shape, dtype)

    scratch = [
        v(tr, t_rows), v(tr, t_rows), v(long, n * 16), v(n * 16, long), v(long, e_n * 16), v(e_n * 16, long),
        v(long, n * 128), v(e_n * 16, n * 128), v(e_n, n * 16, 128), v(e_n * n * 16, 128), v(e_n * 16, n * 128),
        v(e_n * main, width), v(e_n * main, width),
        v(r, w), v(r, w), v(r, w), v(r, w),
        v(w, fh), v(w, fh), v(fh, w),
        v(e_n, 2, q_n, slots, b), v(e_n, 2, 2, slots, b), v(e_n, 2, slots, b),
        v(e_n, q_n, top, b), v(e_n, q_n, bottom, b), v(e_n, 2, top, b), v(e_n, 2, bottom, b),
        v(e_n, top, b), v(e_n, bottom, b),
        v(r, b, dtype=F32), v(r, b, dtype=F32), v(r, b, dtype=F32),
        v(r, ff), v(r, ff), v(r, ff),
        v(r, w), v(r, w), v(tr, width), v(tr, width),
        v(w, r), v(w, ff), v(w, ff), v(ff, w),
        pltpu.SemaphoreType.DMA((3,)),
        pltpu.SemaphoreType.DMA((2, 3)),
        pltpu.SemaphoreType.DMA((6,)),
        pltpu.SemaphoreType.DMA((3, e_n)),
        pltpu.SemaphoreType.DMA((2, n)),
        pltpu.SemaphoreType.DMA((1,)),
        pltpu.SemaphoreType.DMA((10, e_n)),
        pltpu.SemaphoreType.DMA((2, 18, e_n)),
    ]
    mixed, input_grad, gg, gu, gd = pl.pallas_call(
        functools.partial(layer_kernel, n, e_n, cap),
        out_shape=(v(t_rows, width), v(t_rows, width), v(w, ff), v(w, ff), v(ff, w)),
        in_specs=[vm] * 4 + [pl.BlockSpec(memory_space=pl.ANY)] * 3,
        out_specs=(vm,) * 5,
        scratch_shapes=scratch,
        compiler_params=pltpu.CompilerParams(
            collective_id=0, has_side_effects=True, vmem_limit_bytes=54 * 1024 * 1024
        ),
    )(tokens, cotangent, routes.reshape(1, -1), probs.reshape(1, -1), w_gate[0], w_up[0], w_down[0])
    return mixed, input_grad, gg[None], gu[None], gd[None]


def packs(n, e_n, cap, width):
    extra, cbs = cap % 16, width // n // 128
    return (
        n == 8 and cap > 16 and extra > 0 and extra & (extra - 1) == 0 and n & (n - 1) == 0
        and n * extra == 16 and e_n * extra <= 16 and 2 * extra * cbs == 16
    )


def slot_table(routes, experts_all, capacity):
    flat = routes.reshape(-1)
    hits = (flat[:, None] == jnp.arange(experts_all, dtype=jnp.int32)[None, :]).astype(jnp.int32)
    at = jnp.arange(flat.shape[0], dtype=jnp.int32)
    earlier = (at[:, None] > at[None, :]).astype(BF)
    before = nn(earlier, hits.astype(BF)).astype(jnp.int32)
    place = jnp.sum(before * hits, axis=1)
    target = flat * capacity + place
    table = jnp.arange(experts_all * capacity, dtype=jnp.int32)[:, None] == target[None, :]
    return table.astype(jnp.bfloat16)


def spread_rows(table, values, slices):
    shaped = values.reshape(values.shape[0], slices, values.shape[1] // slices)
    return jnp.einsum("st,tnk->nsk", table, shaped, preferred_element_type=jnp.float32).astype(
        jnp.bfloat16
    )


def to_rows(received, local_count):
    sources, slots, width = received.shape
    shaped = received.reshape(sources, local_count, slots // local_count, width)
    shaped = jnp.swapaxes(shaped, 1, 2)
    return shaped.reshape(sources * (slots // local_count), local_count, width)


def to_sources(rowwise, capacity):
    total, local_count, width = rowwise.shape
    shaped = rowwise.reshape(total // capacity, capacity, local_count, width)
    shaped = jnp.swapaxes(shaped, 1, 2)
    return shaped.reshape(total // capacity, local_count * capacity, width)


def collect(table, back, tok_rows, top):
    picked = jnp.einsum("st,nsk->tnk", table, back, preferred_element_type=jnp.float32)
    return picked.reshape(tok_rows, top, -1)


def per_device(tokens, probs, routes, w_gate, w_up, w_down, cotangent):
    local_count = w_gate.shape[0]
    n_dp = lax.axis_size("dp")
    n_exp = lax.axis_size("expert")
    experts_all = local_count * n_exp
    tok_rows, width = tokens.shape
    top = routes.shape[1]
    capacity = max(2, 17 * tok_rows * top // (16 * experts_all))
    ff = w_gate.shape[2]
    if (
        local_count == 1 and top == 1 and n_dp % 2 == 0 and ff % (n_dp * 128) == 0
        and tok_rows % 128 == 0 and width % (n_dp * 128) == 0 and packs(n_dp, n_exp, capacity, width)
    ):
        return fused_layer(
            tokens, probs, routes, w_gate, w_up, w_down, cotangent, n_dp, n_exp, capacity
        )
    blocks = n_dp * n_exp
    slot_width = width // n_dp
    table = slot_table(routes, experts_all, capacity)
    x_send = spread_rows(table, jnp.repeat(tokens, top, axis=0), n_dp)
    x_send = x_send.reshape(blocks, local_count * capacity, slot_width)
    weight = probs.astype(jnp.float32)
    scaled = (jnp.repeat(cotangent, top, axis=0).astype(jnp.float32) * weight).astype(jnp.bfloat16)
    x_got = lax.all_to_all(x_send, ("dp", "expert"), split_axis=0, concat_axis=0, tiled=True)
    rows = to_rows(x_got, local_count)
    part = rows
    gate = jnp.einsum("red,edf->ref", part, w_gate, preferred_element_type=jnp.float32)
    upper = jnp.einsum("red,edf->ref", part, w_up, preferred_element_type=jnp.float32)
    summed = lax.psum_scatter(
        jnp.stack([gate, upper], axis=2).astype(jnp.bfloat16), "dp", scatter_dimension=0, tiled=True
    ).astype(jnp.float32)
    gate_pre = summed[:, :, 0]
    up_value = summed[:, :, 1]
    sig = jax.nn.sigmoid(gate_pre)
    act = (gate_pre * sig * up_value).astype(jnp.bfloat16)
    act_all = lax.all_gather(act, "dp", axis=0, tiled=True)
    result = jnp.einsum("ref,efd->red", act_all, w_down, preferred_element_type=jnp.float32).astype(
        jnp.bfloat16
    )
    outgoing = to_sources(result, capacity)
    back = lax.all_to_all(outgoing, ("dp", "expert"), split_axis=0, concat_axis=0, tiled=True)
    back = back.reshape(n_dp, experts_all * capacity, slot_width)
    picked = collect(table, back, tok_rows, top)
    mixed = jnp.sum(picked * weight[..., None], axis=1).astype(jnp.bfloat16)
    dy_send = spread_rows(table, scaled, n_dp).reshape(blocks, local_count * capacity, slot_width)
    dy_got = lax.all_to_all(dy_send, ("dp", "expert"), split_axis=0, concat_axis=0, tiled=True)
    dout = to_rows(dy_got, local_count)
    grad_down = jnp.einsum("ref,red->efd", act_all, dout, preferred_element_type=jnp.float32)
    part = dout
    dact = lax.psum_scatter(
        jnp.einsum("red,efd->ref", part, w_down, preferred_element_type=jnp.float32).astype(
            jnp.bfloat16
        ),
        "dp",
        scatter_dimension=0,
        tiled=True,
    ).astype(jnp.float32)
    dgate = (dact * up_value * sig * (1.0 + gate_pre * (1.0 - sig))).astype(jnp.bfloat16)
    dup = (dact * gate_pre * sig).astype(jnp.bfloat16)
    dgate_all, dup_all = (
        lax.all_gather(dgate, "dp", axis=0, tiled=True),
        lax.all_gather(dup, "dp", axis=0, tiled=True),
    )
    grad_gate = jnp.einsum("red,ref->edf", rows, dgate_all, preferred_element_type=jnp.float32)
    grad_up = jnp.einsum("red,ref->edf", rows, dup_all, preferred_element_type=jnp.float32)
    slot_grad = jnp.einsum(
        "ref,edf->red", dgate_all, w_gate, preferred_element_type=jnp.float32
    ) + jnp.einsum("ref,edf->red", dup_all, w_up, preferred_element_type=jnp.float32)
    slot_grad = slot_grad.astype(jnp.bfloat16)
    returned = lax.all_to_all(
        to_sources(slot_grad, capacity), ("dp", "expert"), split_axis=0, concat_axis=0, tiled=True
    )
    returned = returned.reshape(n_dp, experts_all * capacity, slot_width)
    input_grad = jnp.sum(collect(table, returned, tok_rows, top), axis=1).astype(jnp.bfloat16)
    return (
        mixed,
        input_grad,
        grad_gate.astype(jnp.bfloat16),
        grad_up.astype(jnp.bfloat16),
        grad_down.astype(jnp.bfloat16),
    )


def solution(mesh):
    return jax.shard_map(
        per_device,
        mesh=mesh,
        in_specs=(
            P(("dp", "expert"), None),
            P(("dp", "expert"), None),
            P(("dp", "expert"), None),
            P("expert", "dp", None),
            P("expert", "dp", None),
            P("expert", None, "dp"),
            P(("dp", "expert"), None),
        ),
        out_specs=(
            P(("dp", "expert"), None),
            P(("dp", "expert"), None),
            P("expert", "dp", None),
            P("expert", "dp", None),
            P("expert", None, "dp"),
        ),
        check_vma=False,
    )
```

```python
import functools

import jax
import jax.numpy as jnp
from jax import lax
from jax.experimental import pallas as pl
from jax.experimental.pallas import tpu as pltpu
from jax.sharding import PartitionSpec as P

BF = jnp.bfloat16
F32 = jnp.float32


def nn(a, b):
    return lax.dot_general(a, b, (((1,), (0,)), ((), ())), preferred_element_type=F32)


def nt(a, b):
    return lax.dot_general(a, b, (((1,), (1,)), ((), ())), preferred_element_type=F32)


def tn(a, b):
    return lax.dot_general(a, b, (((0,), (0,)), ((), ())), preferred_element_type=F32)


def flat_bits(value):
    return value.bit_length() - 1


def layer_kernel(
    n, e_n, cap,
    tok, cot, route, prob, wg_h, wu_h, wd_h,
    yb, sb, tab, tabw, gg_o, gu_o, gd_o,
    pn, pnt, pe, pet, st, te, tiles, et, eb,
    xs, ds_, xr, dr, xp, dp, pwg, pwu, pwd,
    gs, gr, gt, hst, hsb, hrt, hrb, htt, htb, dsum, pre, upv, act, dga, dua, rs, ss, x_t, wg, wu, wd,
    sem_own, sem_pw, sem_out, sem_in, sem_back, sem_ext, sem_ps, sem_q,
):
    m = lax.axis_index("dp")
    z = lax.axis_index("expert")
    q_n = n // 2
    q = m // 2
    c = lax.rem(m, 2)
    pm = m + 1 - 2 * c
    on_x, on_y = lax.rem(q, 2), q // 2
    qx, qy = q + 1 - 2 * on_x, q + 2 - 4 * on_y
    mx, my = 2 * qx + c, 2 * qy + c
    slots = n * cap
    top = (slots // 16 + 1) // 2 * 16
    bottom = slots - top
    main = cap // 16 * 16
    extra = cap - main
    em, nm = e_n * main, n * main
    t_rows, w = tok.shape[0], tok.shape[1] // n
    cbs = w // 128
    ff = wg_h.shape[1]
    fh = ff // 2
    b = fh // q_n

    def span(start, size, unit):
        return pl.ds(pl.multiple_of(start, unit), size)

    def rows(k):
        return span(k * slots, slots, 16)

    def mains(k, i):
        return span(k * slots + i * main, main, 16)

    def uppers(k):
        return span(k * slots, top, 16)

    def lowers(k):
        return span(k * slots + top, bottom, 16)

    def chunk_mains(k):
        return span(k * slots, nm, 16)

    def chunk_extras(k):
        return span(k * slots + nm, 16, 16)

    def places(e):
        return span(e * main, main, 16)

    def cols(k):
        return span(k * w, w, 128)

    def lanes(k):
        return span(k * 128, 128, 128)

    def tile(k):
        return span(k * 16, 16, 16)

    my_half = span(c * fh, fh, 128)
    other_half = span((1 - c) * fh, fh, 128)

    def block(qq):
        return span(c * fh + qq * b, b, 128)

    def copy(src, dst, send, recv, dp_at, ex_at):
        return pltpu.make_async_remote_copy(
            src_ref=src, dst_ref=dst, send_sem=send, recv_sem=recv,
            device_id=(dp_at, ex_at), device_id_type=pl.DeviceIdType.MESH,
        )

    def near(d):
        upper = (2 * z) // e_n
        low = z + upper * (e_n - 1 - 2 * z)
        side = 2 * lax.rem(d, 2) - 1
        at = jnp.where(d <= 2 * low, low + side * ((d + 1) // 2), d)
        return at + upper * (e_n - 1 - 2 * at)

    def back(d):
        return near(0 if d == 0 else e_n - d)

    def ways(i):
        to_left = on_x if i % 2 == 0 else 1 - on_x
        to_up = on_y if i // 2 == 0 else 1 - on_y
        return 2 * to_left + to_up, 2 * to_up + to_left

    def loop(lo, hi, body):
        def step(i, carry):
            body(i)
            return carry

        lax.fori_loop(lo, hi, step, 0)

    def partner(at, d, size):
        if size & (size - 1):
            return lax.rem(at + d, size)
        other, step = at, 1
        while step < size:
            if d & step:
                other = other + step - 2 * step * lax.rem(at // step, 2)
            step *= 2
        return other

    def to_plane(e, pairs):
        @pl.when(e != z)
        def _():
            for out, _ in pairs:
                out(m, e).start()

        @pl.when(e == z)
        def _():
            for _, own in pairs:
                own.start()

        for d in range(1, n):
            for out, _ in pairs:
                out(partner(m, d, n), e).start()

    def x_out(i, e):
        return copy(xs.at[places(e), cols(i)], xr.at[mains(z, m), :], sem_out.at[0], sem_in.at[0, z], i, e)

    x_own = pltpu.make_async_copy(xs.at[places(z), cols(m)], xr.at[mains(z, m), :], sem_in.at[0, z])

    def d_out(i, e):
        return copy(ds_.at[places(e), cols(i)], dr.at[mains(z, m), :], sem_out.at[1], sem_in.at[1, z], i, e)

    d_own = pltpu.make_async_copy(ds_.at[places(z), cols(m)], dr.at[mains(z, m), :], sem_in.at[1, z])

    def t_out(i, e):
        return copy(te.at[tile(e), lanes(i)], tiles.at[z, tile(m), :], sem_out.at[2], sem_in.at[2, z], i, e)

    t_own = pltpu.make_async_copy(te.at[tile(z), lanes(m)], tiles.at[z, tile(m), :], sem_in.at[2, z])

    def y_out(i, k):
        return copy(rs.at[mains(k, i), :], yb.at[places(z), cols(m)], sem_out.at[3], sem_back.at[0, m], i, k)

    y_own = pltpu.make_async_copy(rs.at[mains(z, m), :], yb.at[places(z), cols(m)], sem_back.at[0, m])

    def s_out(i, k):
        return copy(ss.at[mains(k, i), :], sb.at[places(z), cols(m)], sem_out.at[4], sem_back.at[1, m], i, k)

    s_own = pltpu.make_async_copy(ss.at[mains(z, m), :], sb.at[places(z), cols(m)], sem_back.at[1, m])

    def e_out_(i, k):
        return copy(et.at[tile(k * n + i), :], eb.at[tile(z), lanes(m)], sem_out.at[5], sem_ext.at[0], i, k)

    e_own = pltpu.make_async_copy(et.at[tile(z * n + m), :], eb.at[tile(z), lanes(m)], sem_ext.at[0])

    def arrived(ref, sem):
        copy(ref, ref, sem, sem, pm, z).wait_recv()

    def sent(ref, sem):
        copy(ref, ref, sem, sem, pm, z).wait_send()

    def pass_pair(no, src, dst):
        def out(k):
            return copy(src(k), dst(k), sem_ps.at[2 * no, k], sem_ps.at[2 * no + 1, k], pm, z)

        return out

    xf = pass_pair(0, lambda k: xr.at[rows(k)], lambda k: xp.at[rows(k)])
    df = pass_pair(1, lambda k: dr.at[rows(k)], lambda k: dp.at[rows(k)])

    def half_pass(no, ref):
        send, recv = sem_ps.at[2 * no], sem_ps.at[2 * no + 1]

        def out(k):
            part = ref.at[rows(k), my_half]
            return copy(part, part, send.at[k], recv.at[k], pm, z)

        def got(k):
            part = ref.at[rows(k), other_half]
            return copy(part, part, send.at[k], recv.at[k], pm, z)

        return out, got

    af_out, af_got = half_pass(2, act)
    ef_out, ef_got = half_pass(3, dga)
    uf_out, uf_got = half_pass(4, dua)

    def to_x(no, src, dst):
        return lambda k: copy(src(k), dst(k), sem_q.at[0, no, k], sem_q.at[1, no, k], mx, z)

    def to_y(no, src, dst):
        return lambda k: copy(src(k), dst(k), sem_q.at[0, no, k], sem_q.at[1, no, k], my, z)

    def same(no, to, part):
        return to(no, part, part)

    g1 = (
        to_x(0, lambda k: gs.at[k, 0, 2:4], lambda k: gr.at[k, 0]),
        to_y(1, lambda k: gs.at[k, 1, 2:4], lambda k: gr.at[k, 1]),
    )
    g2 = (
        to_y(2, lambda k: gs.at[k, 0, 1], lambda k: gt.at[k, 0]),
        to_x(3, lambda k: gs.at[k, 1, 1], lambda k: gt.at[k, 1]),
    )
    h1 = (
        to_x(4, lambda k: hst.at[k, 2:4], lambda k: hrt.at[k]),
        to_y(5, lambda k: hsb.at[k, 2:4], lambda k: hrb.at[k]),
    )
    h2 = (
        to_y(6, lambda k: hst.at[k, 1], lambda k: htt.at[k]),
        to_x(7, lambda k: hsb.at[k, 1], lambda k: htb.at[k]),
    )
    a1 = (
        same(8, to_x, lambda k: act.at[rows(k), block(q)]),
        same(9, to_y, lambda k: act.at[rows(k), block(q)]),
    )
    a2 = (
        same(10, to_y, lambda k: act.at[uppers(k), block(qx)]),
        same(11, to_x, lambda k: act.at[lowers(k), block(qy)]),
    )
    e1 = (
        same(12, to_x, lambda k: dga.at[rows(k), block(q)]),
        same(13, to_y, lambda k: dga.at[rows(k), block(q)]),
    )
    u1 = (
        same(14, to_x, lambda k: dua.at[rows(k), block(q)]),
        same(15, to_y, lambda k: dua.at[rows(k), block(q)]),
    )
    e2 = same(16, to_y, lambda k: dga.at[rows(k), block(qx)])
    u2 = same(17, to_x, lambda k: dua.at[rows(k), block(qy)])
    pw = [
        copy(wg_h.at[:, other_half], pwg, sem_pw.at[0, 0], sem_pw.at[1, 0], pm, z),
        copy(wu_h.at[:, other_half], pwu, sem_pw.at[0, 1], sem_pw.at[1, 1], pm, z),
        copy(wd_h.at[other_half], pwd, sem_pw.at[0, 2], sem_pw.at[1, 2], pm, z),
    ]
    own = [
        pltpu.make_async_copy(src, dst, sem_own.at[i])
        for i, (src, dst) in enumerate(((wg_h, wg), (wu_h, wu), (wd_h, wd)))
    ]
    for one in own:
        one.start()
    barrier = pltpu.get_barrier_semaphore()
    here = m * e_n + z

    def greet(d):
        other = lax.rem(here + d, n * e_n)
        pl.semaphore_signal(
            barrier, inc=1, device_id=(other // e_n, lax.rem(other, e_n)),
            device_id_type=pl.DeviceIdType.MESH,
        )

    loop(1, n * e_n, greet)

    name = route[...]
    share = prob[...].astype(F32)
    hits = jnp.where(lax.broadcasted_iota(jnp.int32, (16, t_rows), 0) == name, 1.0, 0.0)
    earlier = jnp.where(
        lax.broadcasted_iota(jnp.int32, (t_rows, t_rows), 0)
        < lax.broadcasted_iota(jnp.int32, (t_rows, t_rows), 1), 1.0, 0.0,
    ).astype(BF)
    place = jnp.sum(nn(hits.astype(BF), earlier) * hits, axis=0, keepdims=True).astype(jnp.int32)
    target = jnp.where(
        place < main, name * main + place, em + name * extra + place - main
    )
    hit = lax.broadcasted_iota(jnp.int32, (em + 16, t_rows), 0) == target
    tab[...] = jnp.where(hit, 1.0, 0.0).astype(BF)
    tabw[...] = jnp.where(hit, share, 0.0).astype(BF)

    def packing(count, flip):
        shape = (count * 16, 2 * cbs * 16) if flip else (2 * cbs * 16, count * 16)
        long = lax.broadcasted_iota(jnp.int32, shape, 1 if flip else 0)
        packed = lax.broadcasted_iota(jnp.int32, shape, 0 if flip else 1)
        slot = long & 15
        group = long >> 4
        want = ((slot >> flat_bits(extra)) << 4) + group * extra + (slot & (extra - 1))
        return jnp.where((packed == want) & (slot < count * extra), 1.0, 0.0).astype(BF)

    def gather(table, src, dst, a):
        for i in range(n):
            at = slice(i * w, (i + 1) * w)
            part = nn(table[...], src[:, at]).astype(BF)
            dst[:, at] = part[:em]
            for cb in range(cbs):
                g = (a * cbs + cb) * 16
                st[g:g + 16, i * 128:(i + 1) * 128] = part[em:, cb * 128:(cb + 1) * 128]

    gather(tab, tok, xs, 0)
    pl.semaphore_wait(barrier, n * e_n - 1)
    to_plane(z, [(x_out, x_own)])
    gather(tabw, cot, ds_, 1)
    pet[...] = packing(e_n, True)
    te[...] = nn(pet[...], st[...]).astype(BF)
    to_plane(z, [(t_out, t_own)])
    loop(1, e_n, lambda d: to_plane(near(d), [(x_out, x_own), (t_out, t_own)]))
    for one in pw:
        one.start()
    pn[...] = packing(n, False)
    pnt[...] = packing(n, True)
    pe[...] = packing(e_n, False)
    for one in own:
        one.wait()
    for one in pw:
        one.wait_recv()

    def x_in(k):
        arrived(tiles.at[k], sem_in.at[2, k])
        spare = nn(pn[...], tiles[k]).astype(BF)
        for cb in range(cbs):
            at = slice(cb * 128, (cb + 1) * 128)
            xr[chunk_extras(k), at] = spare[cb * 16:(cb + 1) * 16]
            dr[chunk_extras(k), at] = spare[(cbs + cb) * 16:(cbs + cb + 1) * 16]
        arrived(xr.at[chunk_mains(k)], sem_in.at[0, k])
        xf(k).start()

    def gate_up(k):
        mine = [nn(xr[rows(k), :], own_w[:, my_half]) for own_w in (wg, wu)]
        xf(k).wait_recv()
        for at, other_w in ((0, pwg), (1, pwu)):
            part = (mine[at] + nn(xp[rows(k), :], other_w[...])).astype(BF)
            for i in range(q_n):
                gs[k, at, ways(i)[at]] = part[:, i * b:(i + 1) * b]
            g1[at](k).start()

    def gate_mid(k):
        for at, keep in ((0, pre), (1, upv)):
            g1[at](k).wait_recv()
            gs[k, at, 1] = (gs[k, at, 1].astype(F32) + gr[k, at, 1].astype(F32)).astype(BF)
            g2[at](k).start()
            keep[rows(k), :] = gs[k, at, 0].astype(F32) + gr[k, at, 0].astype(F32)

    def dout_send(k):
        to_plane(k, [(d_out, d_own)])

    def activate(k):
        for one in g2:
            one(k).wait_recv()
        gate = pre[rows(k), :] + gt[k, 0].astype(F32)
        up = upv[rows(k), :] + gt[k, 1].astype(F32)
        act[rows(k), block(q)] = (gate * jax.nn.sigmoid(gate) * up).astype(BF)
        for one in a1:
            one(k).start()
        pre[rows(k), :] = gate
        upv[rows(k), :] = up

    def act_on(k):
        for near_one, on in zip(a1, a2):
            near_one(k).wait_recv()
            on(k).start()

    def act_pass(k):
        for one in a2:
            one(k).wait_recv()
        af_out(k).start()

    def result_rows(k):
        af_got(k).wait_recv()
        rs[rows(k), :] = nn(act[rows(k), :], wd[...]).astype(BF)
        to_plane(k, [(y_out, y_own)])

    def d_in(k):
        arrived(dr.at[chunk_mains(k)], sem_in.at[1, k])
        df(k).start()

    def down(k):
        mine = nt(dr[rows(k), :], wd[my_half, :])
        df(k).wait_recv()
        part = (mine + nt(dp[rows(k), :], pwd[...])).astype(BF)
        for i in range(q_n):
            at = slice(i * b, (i + 1) * b)
            hst[k, ways(i)[0]] = part[:top, at]
            hsb[k, ways(i)[1]] = part[top:, at]
        for one in h1:
            one(k).start()

    def down_mid(k):
        for first, then, had, got, place in ((h1[0], h2[0], hst, hrt, uppers), (h1[1], h2[1], hsb, hrb, lowers)):
            first(k).wait_recv()
            had[k, 1] = (had[k, 1].astype(F32) + got[k, 1].astype(F32)).astype(BF)
            then(k).start()
            dsum[place(k), :] = had[k, 0].astype(F32) + got[k, 0].astype(F32)

    def act_grad(k):
        for then, got, place in ((h2[0], htt, uppers), (h2[1], htb, lowers)):
            then(k).wait_recv()
            total = dsum[place(k), :] + got[k].astype(F32)
            gate, up = pre[place(k), :], upv[place(k), :]
            sig = jax.nn.sigmoid(gate)
            dga[place(k), block(q)] = (total * up * sig * (1.0 + gate * (1.0 - sig))).astype(BF)
            dua[place(k), block(q)] = (total * gate * sig).astype(BF)
        for one in (*e1, *u1):
            one(k).start()

    def grad_on(k):
        e1[0](k).wait_recv()
        e2(k).start()
        u1[1](k).wait_recv()
        u2(k).start()

    def handed(k):
        e1[1](k).wait_recv()
        e2(k).wait_recv()
        ef_out(k).start()
        u1[0](k).wait_recv()
        u2(k).wait_recv()
        uf_out(k).start()

    def input_grad(k):
        ef_got(k).wait_recv()
        uf_got(k).wait_recv()
        ss[rows(k), :] = (nt(dga[rows(k), :], wg[...]) + nt(dua[rows(k), :], wu[...])).astype(BF)
        to_plane(k, [(s_out, s_own)])
        long = [
            buf[chunk_extras(k), cb * 128:(cb + 1) * 128] for buf in (rs, ss) for cb in range(cbs)
        ]
        et[span(k * n * 16, n * 16, 16), :] = nn(pnt[...], jnp.concatenate(long, axis=0)).astype(BF)
        to_plane(k, [(e_out_, e_own)])

    ahead = (
        (gate_mid, 1, 0), (x_in, 0, 1), (act_on, 2, 2), (gate_up, 0, 4),
        (activate, 1, 7), (act_pass, 2, 8), (result_rows, 3, 10),
    )
    behind = (
        (down_mid, 3, 3), (d_in, 2, 6), (grad_on, 4, 9), (down, 2, 11), (act_grad, 3, 12), (handed, 4, 13), (input_grad, 5, 14),
    )
    plan = []
    for d in range(e_n):
        plan += [(d + lag, at, body, near(d)) for body, lag, at in ahead]
        plan += [(lag + (d and d + 1), at, body, back(d)) for body, lag, at in behind]
        plan += [(d and e_n - 1, 5 + d / 100, dout_send, back(d))]
    for _, _, body, k in sorted(plan, key=lambda one: one[:2]):
        body(k)

    x_t[...] = xr[...].T
    wide = 2 * b

    def down_grad(j):
        at = span(j * wide, wide, 128)
        gd_o[at, :] = tn(act[:, at], dr[...]).astype(BF)

    loop(0, ff // wide, down_grad)

    def weight_grad(j):
        at = span(j * wide, wide, 128)
        gg_o[:, at] = nn(x_t[...], dga[:, at]).astype(BF)
        gu_o[:, at] = nn(x_t[...], dua[:, at]).astype(BF)

    loop(0, ff // wide, weight_grad)

    arrived(eb, sem_ext.at[0])
    spare = nn(pe[...], eb[...]).astype(BF)
    for a, buf in ((0, yb), (1, sb)):
        for cb in range(cbs):
            g = (a * cbs + cb) * 16
            for i in range(n):
                buf[em:em + 16, i * w + cb * 128:i * w + (cb + 1) * 128] = spare[g:g + 16, i * 128:(i + 1) * 128]

    for a, buf in ((0, yb), (1, sb)):
        for i in range(n):
            arrived(buf.at[0:em, cols(i)], sem_back.at[a, i])

    for at in (0, 1, 3, 4):
        sent(xr.at[0:(n * e_n - 1) * main], sem_out.at[at])
    for at in (2, 5):
        sent(et.at[0:(n * e_n - 1) * 16], sem_out.at[at])
    for one in pw:
        one.wait_send()

    def chunk_end(k):
        for out in (xf, df, af_out, ef_out, uf_out):
            out(k).wait_send()
        for out in (*g1, *g2, *h1, *h2, *a1, *a2, *e1, *u1, e2, u2):
            out(k).wait_send()

    loop(0, e_n, chunk_end)


def write_out(n, yb, sb, tab, tabw, gg, gu, gd, mix_o, ig_o, gg_o, gu_o, gd_o, mixed, back, sem_grad, sem_row):
    copies = [
        pltpu.make_async_copy(src, dst, sem_grad.at[i])
        for i, (src, dst) in enumerate(((gg, gg_o), (gu, gu_o), (gd, gd_o)))
    ]
    for one in copies:
        one.start()
    w = yb.shape[1] // n
    for a, (table, rows, out, dst) in enumerate(((tabw, yb, mixed, mix_o), (tab, sb, back, ig_o))):
        for i in range(n):
            at = slice(i * w, (i + 1) * w)
            out[:, at] = tn(table[...], rows[:, at]).astype(BF)
            one = pltpu.make_async_copy(out.at[:, at], dst.at[:, at], sem_row.at[a, i])
            one.start()
            copies.append(one)
    for one in copies:
        one.wait()


def fused_layer(tokens, probs, routes, w_gate, w_up, w_down, cotangent, n, e_n, cap):
    t_rows, width = tokens.shape
    w = width // n
    ff = w_gate.shape[2]
    slots, fh, q_n = n * cap, ff // 2, n // 2
    b = fh // q_n
    r = e_n * slots
    main = cap // 16 * 16
    top = (slots // 16 + 1) // 2 * 16
    bottom = slots - top
    tr, cbs = e_n * main + 16, w // 128
    long = 2 * cbs * 16
    vm = pl.BlockSpec(memory_space=pltpu.VMEM)

    def v(*shape, dtype=BF):
        return pltpu.VMEM(shape, dtype)

    scratch = [
        v(long, n * 16), v(n * 16, long), v(long, e_n * 16), v(e_n * 16, long),
        v(long, n * 128), v(e_n * 16, n * 128), v(e_n, n * 16, 128), v(e_n * n * 16, 128), v(e_n * 16, n * 128),
        v(e_n * main, width), v(e_n * main, width),
        v(r, w), v(r, w), v(r, w), v(r, w),
        v(w, fh), v(w, fh), v(fh, w),
        v(e_n, 2, q_n, slots, b), v(e_n, 2, 2, slots, b), v(e_n, 2, slots, b),
        v(e_n, q_n, top, b), v(e_n, q_n, bottom, b), v(e_n, 2, top, b), v(e_n, 2, bottom, b),
        v(e_n, top, b), v(e_n, bottom, b),
        v(r, b, dtype=F32), v(r, b, dtype=F32), v(r, b, dtype=F32),
        v(r, ff), v(r, ff), v(r, ff),
        v(r, w), v(r, w),
        v(w, r), v(w, ff), v(w, ff), v(ff, w),
        pltpu.SemaphoreType.DMA((3,)),
        pltpu.SemaphoreType.DMA((2, 3)),
        pltpu.SemaphoreType.DMA((6,)),
        pltpu.SemaphoreType.DMA((3, e_n)),
        pltpu.SemaphoreType.DMA((2, n)),
        pltpu.SemaphoreType.DMA((1,)),
        pltpu.SemaphoreType.DMA((10, e_n)),
        pltpu.SemaphoreType.DMA((2, 18, e_n)),
    ]
    held = pl.pallas_call(
        functools.partial(layer_kernel, n, e_n, cap),
        out_shape=(
            v(tr, width), v(tr, width), v(tr, t_rows), v(tr, t_rows), v(w, ff), v(w, ff), v(ff, w),
        ),
        in_specs=[vm] * 4 + [pl.BlockSpec(memory_space=pl.ANY)] * 3,
        out_specs=(vm,) * 7,
        scratch_shapes=scratch,
        compiler_params=pltpu.CompilerParams(
            collective_id=0, has_side_effects=True, vmem_limit_bytes=54 * 1024 * 1024
        ),
    )(tokens, cotangent, routes.reshape(1, -1), probs.reshape(1, -1), w_gate[0], w_up[0], w_down[0])
    held = tuple(pltpu.with_memory_space_constraint(one, pltpu.VMEM) for one in held)
    mixed, input_grad, gg, gu, gd = pl.pallas_call(
        functools.partial(write_out, n),
        out_shape=tuple(
            jax.ShapeDtypeStruct(shape, BF)
            for shape in ((t_rows, width), (t_rows, width), (w, ff), (w, ff), (ff, w))
        ),
        in_specs=[vm] * len(held),
        out_specs=(pl.BlockSpec(memory_space=pl.ANY),) * 5,
        scratch_shapes=[
            v(t_rows, width), v(t_rows, width),
            pltpu.SemaphoreType.DMA((3,)), pltpu.SemaphoreType.DMA((2, n)),
        ],
        compiler_params=pltpu.CompilerParams(vmem_limit_bytes=8 * 1024 * 1024),
    )(*held)
    return mixed, input_grad, gg[None], gu[None], gd[None]


def packs(n, e_n, cap, width):
    extra, cbs = cap % 16, width // n // 128
    return (
        n == 8 and cap > 16 and extra > 0 and extra & (extra - 1) == 0 and n & (n - 1) == 0
        and n * extra == 16 and e_n * extra <= 16 and 2 * extra * cbs == 16
    )


def slot_table(routes, experts_all, capacity):
    flat = routes.reshape(-1)
    hits = (flat[:, None] == jnp.arange(experts_all, dtype=jnp.int32)[None, :]).astype(jnp.int32)
    at = jnp.arange(flat.shape[0], dtype=jnp.int32)
    earlier = (at[:, None] > at[None, :]).astype(BF)
    before = nn(earlier, hits.astype(BF)).astype(jnp.int32)
    place = jnp.sum(before * hits, axis=1)
    target = flat * capacity + place
    table = jnp.arange(experts_all * capacity, dtype=jnp.int32)[:, None] == target[None, :]
    return table.astype(jnp.bfloat16)


def spread_rows(table, values, slices):
    shaped = values.reshape(values.shape[0], slices, values.shape[1] // slices)
    return jnp.einsum("st,tnk->nsk", table, shaped, preferred_element_type=jnp.float32).astype(
        jnp.bfloat16
    )


def to_rows(received, local_count):
    sources, slots, width = received.shape
    shaped = received.reshape(sources, local_count, slots // local_count, width)
    shaped = jnp.swapaxes(shaped, 1, 2)
    return shaped.reshape(sources * (slots // local_count), local_count, width)


def to_sources(rowwise, capacity):
    total, local_count, width = rowwise.shape
    shaped = rowwise.reshape(total // capacity, capacity, local_count, width)
    shaped = jnp.swapaxes(shaped, 1, 2)
    return shaped.reshape(total // capacity, local_count * capacity, width)


def collect(table, back, tok_rows, top):
    picked = jnp.einsum("st,nsk->tnk", table, back, preferred_element_type=jnp.float32)
    return picked.reshape(tok_rows, top, -1)


def per_device(tokens, probs, routes, w_gate, w_up, w_down, cotangent):
    local_count = w_gate.shape[0]
    n_dp = lax.axis_size("dp")
    n_exp = lax.axis_size("expert")
    experts_all = local_count * n_exp
    tok_rows, width = tokens.shape
    top = routes.shape[1]
    capacity = max(2, 17 * tok_rows * top // (16 * experts_all))
    ff = w_gate.shape[2]
    if (
        local_count == 1 and top == 1 and n_dp % 2 == 0 and ff % (n_dp * 128) == 0
        and tok_rows % 128 == 0 and width % (n_dp * 128) == 0 and packs(n_dp, n_exp, capacity, width)
    ):
        return fused_layer(
            tokens, probs, routes, w_gate, w_up, w_down, cotangent, n_dp, n_exp, capacity
        )
    blocks = n_dp * n_exp
    slot_width = width // n_dp
    table = slot_table(routes, experts_all, capacity)
    x_send = spread_rows(table, jnp.repeat(tokens, top, axis=0), n_dp)
    x_send = x_send.reshape(blocks, local_count * capacity, slot_width)
    weight = probs.astype(jnp.float32)
    scaled = (jnp.repeat(cotangent, top, axis=0).astype(jnp.float32) * weight).astype(jnp.bfloat16)
    x_got = lax.all_to_all(x_send, ("dp", "expert"), split_axis=0, concat_axis=0, tiled=True)
    rows = to_rows(x_got, local_count)
    part = rows
    gate = jnp.einsum("red,edf->ref", part, w_gate, preferred_element_type=jnp.float32)
    upper = jnp.einsum("red,edf->ref", part, w_up, preferred_element_type=jnp.float32)
    summed = lax.psum_scatter(
        jnp.stack([gate, upper], axis=2).astype(jnp.bfloat16), "dp", scatter_dimension=0, tiled=True
    ).astype(jnp.float32)
    gate_pre = summed[:, :, 0]
    up_value = summed[:, :, 1]
    sig = jax.nn.sigmoid(gate_pre)
    act = (gate_pre * sig * up_value).astype(jnp.bfloat16)
    act_all = lax.all_gather(act, "dp", axis=0, tiled=True)
    result = jnp.einsum("ref,efd->red", act_all, w_down, preferred_element_type=jnp.float32).astype(
        jnp.bfloat16
    )
    outgoing = to_sources(result, capacity)
    back = lax.all_to_all(outgoing, ("dp", "expert"), split_axis=0, concat_axis=0, tiled=True)
    back = back.reshape(n_dp, experts_all * capacity, slot_width)
    picked = collect(table, back, tok_rows, top)
    mixed = jnp.sum(picked * weight[..., None], axis=1).astype(jnp.bfloat16)
    dy_send = spread_rows(table, scaled, n_dp).reshape(blocks, local_count * capacity, slot_width)
    dy_got = lax.all_to_all(dy_send, ("dp", "expert"), split_axis=0, concat_axis=0, tiled=True)
    dout = to_rows(dy_got, local_count)
    grad_down = jnp.einsum("ref,red->efd", act_all, dout, preferred_element_type=jnp.float32)
    part = dout
    dact = lax.psum_scatter(
        jnp.einsum("red,efd->ref", part, w_down, preferred_element_type=jnp.float32).astype(
            jnp.bfloat16
        ),
        "dp",
        scatter_dimension=0,
        tiled=True,
    ).astype(jnp.float32)
    dgate = (dact * up_value * sig * (1.0 + gate_pre * (1.0 - sig))).astype(jnp.bfloat16)
    dup = (dact * gate_pre * sig).astype(jnp.bfloat16)
    dgate_all, dup_all = (
        lax.all_gather(dgate, "dp", axis=0, tiled=True),
        lax.all_gather(dup, "dp", axis=0, tiled=True),
    )
    grad_gate = jnp.einsum("red,ref->edf", rows, dgate_all, preferred_element_type=jnp.float32)
    grad_up = jnp.einsum("red,ref->edf", rows, dup_all, preferred_element_type=jnp.float32)
    slot_grad = jnp.einsum(
        "ref,edf->red", dgate_all, w_gate, preferred_element_type=jnp.float32
    ) + jnp.einsum("ref,edf->red", dup_all, w_up, preferred_element_type=jnp.float32)
    slot_grad = slot_grad.astype(jnp.bfloat16)
    returned = lax.all_to_all(
        to_sources(slot_grad, capacity), ("dp", "expert"), split_axis=0, concat_axis=0, tiled=True
    )
    returned = returned.reshape(n_dp, experts_all * capacity, slot_width)
    input_grad = jnp.sum(collect(table, returned, tok_rows, top), axis=1).astype(jnp.bfloat16)
    return (
        mixed,
        input_grad,
        grad_gate.astype(jnp.bfloat16),
        grad_up.astype(jnp.bfloat16),
        grad_down.astype(jnp.bfloat16),
    )


def solution(mesh):
    return jax.shard_map(
        per_device,
        mesh=mesh,
        in_specs=(
            P(("dp", "expert"), None),
            P(("dp", "expert"), None),
            P(("dp", "expert"), None),
            P("expert", "dp", None),
            P("expert", "dp", None),
            P("expert", None, "dp"),
            P(("dp", "expert"), None),
        ),
        out_specs=(
            P(("dp", "expert"), None),
            P(("dp", "expert"), None),
            P("expert", "dp", None),
            P("expert", "dp", None),
            P("expert", None, "dp"),
        ),
        check_vma=False,
    )
```
